512 devices in a mesh: tok: 64 (over z, y), ch: 8 (over x, core).
Axes of the slice: x: 4, y: 8, z: 8, core: 2. Of those that a mesh axis runs over, the one named last changes fastest.
Arguments:
- hidden: bfloat16 [8192, 1024], P('tok'), may hold values from -13 to 13
- pre_gates: bfloat16 [2, 8192, 1024], P(None, 'tok', 'ch'), may hold values from -6 to 6
- conv_weight: bfloat16 [2, 4, 1024, 1024], P(None, None, 'tok', 'ch'), may hold values from -0.09375 to 0.09375
- head_weight: bfloat16 [1024, 20480], P('tok', 'ch'), may hold values from -8 to 8
- cluster_weight: bfloat16 [1024, 128], P('tok', 'ch'), may hold values from -0.59765625 to 0.59765625
- tail1_proj: bfloat16 [64, 1024, 256], P('tok'), may hold values from -1 to 1
- tail2_proj: bfloat16 [64, 1024, 64], P('tok'), may hold values from -1 to 1
- tail1_out: bfloat16 [64, 256, 3072], P('tok', None, 'ch'), may hold values from -12 to 12
- tail2_out: bfloat16 [64, 64, 9216], P('tok', None, 'ch'), may hold values from -30 to 30
- cluster_id: int32 [8192], P('tok'), may hold values from -1 to 127, as said below
- target: int32 [8192], P('tok'), may hold values from 0 to 20479, as said below
Outputs:
- token_loss: float32 [8192], P('tok')
- grad_input: bfloat16 [8192, 1024], P('tok', 'ch')
- proj1_grad: float32 [64, 1024, 256], P('tok', 'ch')
- proj2_grad: float32 [64, 1024, 64], P('tok', 'ch')
- out1_grad: float32 [64, 256, 3072], P('tok', None, 'ch')
- out2_grad: float32 [64, 64, 9216], P('tok', None, 'ch')
The draws below stay inside these ranges and needn't reach their ends.
Inputs may be any that keep to these rules, and one draw needn't show every extreme that they name: `cluster_id`: in each aligned block of 128 tokens at most 2 name clusters of one owner; in every draw one owner is named by 2 tokens of every block, and every owner by 2 tokens of some block. `target`: below 20480 for a head token, below 3072 for a first-tier token, below 9216 for a second-tier token.
All inputs are finite; a program needn't handle non-finite values.
Results may differ from the reference program's by a relative error of at most 0.01.
Values may be sent and summed in bfloat16 or wider, within the bound.
No kernel may reach another device: no remote copies, remote signals or barrier semaphores. Data moves between devices by JAX's collectives and lax.ppermute only.
A program may use at most 64 MiB of HBM per device.

```python
import math
import jax
import jax.numpy as jnp
from jax import lax

D = 1024
HEAD = 20480
P1 = 256
P2 = 64
W1 = 3072
W2 = 9216
K = 4
LEN = 128
TOK_DEV = 128
OWNERS = 64
TOKENS = 8192
CAP = 2
SLOTS = 128
CLUST = 128
N_TOK = 64
N_CH = 8


def routing(key):
    key_list = jax.random.split(jax.random.fold_in(key, 101), 6)
    full_owner = jax.random.randint(key_list[0], (), 0, OWNERS)
    shift_owner = jax.random.randint(key_list[1], (), 0, OWNERS)
    blocks = jnp.arange(OWNERS, dtype=jnp.int32)
    chosen = (blocks + shift_owner) % OWNERS
    orders = jax.vmap(lambda block_key: jax.random.permutation(block_key, TOK_DEV))(jax.random.split(key_list[2], OWNERS)).astype(jnp.int32)
    position = jnp.arange(TOK_DEV, dtype=jnp.int32)[None, :]
    forced_full = jnp.broadcast_to(position < CAP, (OWNERS, TOK_DEV))
    forced_own = (position >= CAP) & (position < 2 * CAP) & (chosen[:, None] != full_owner)
    random_tail = jax.random.randint(key_list[3], (OWNERS, TOK_DEV), 0, 2) == 1
    random_owner = jax.random.randint(key_list[4], (OWNERS, TOK_DEV), 0, OWNERS)
    random_tier = jax.random.randint(key_list[5], (OWNERS, TOK_DEV), 0, 2)
    owner_ids = jnp.where(forced_full, full_owner, jnp.where(forced_own, chosen[:, None], random_owner))
    tier_ids = jnp.where(forced_full | forced_own, position % 2, random_tier)
    wanted = forced_full | forced_own | random_tail
    hits = ((owner_ids[:, :, None] == blocks[None, None, :]) & wanted[:, :, None]).astype(jnp.int32)
    running = jnp.cumsum(hits, axis=1)
    rank = jnp.sum(running * hits, axis=2) - 1
    kept = wanted & (rank < CAP)
    cluster_order = jnp.where(kept, 2 * owner_ids + tier_ids, -1).astype(jnp.int32)
    row_index = blocks[:, None]
    cluster = jnp.zeros((OWNERS, TOK_DEV), jnp.int32).at[row_index, orders].set(cluster_order)
    return (cluster.reshape(TOKENS), orders, full_owner, shift_owner)


def aligned(key):
    cluster, orders, full_owner, shift_owner = routing(key)
    owner_range = jnp.arange(OWNERS, dtype=jnp.int32)
    is_full = owner_range == full_owner
    block = jnp.where(is_full, 0, (owner_range - shift_owner) % OWNERS)
    parity = CAP % 2
    first_pos = jnp.where(is_full, 0, CAP + parity)
    second_pos = jnp.where(is_full, 1, CAP + 1 - parity)
    first_tok = block * TOK_DEV + orders[block, first_pos]
    second_tok = block * TOK_DEV + orders[block, second_pos]
    head_tok = jax.random.randint(jax.random.fold_in(key, 303), (8,), 0, TOKENS)
    return (first_tok, second_tok, head_tok)


def hidden_rows(key):
    key_list = jax.random.split(jax.random.fold_in(key, 404), 3)
    first_tok, second_tok, head_tok = aligned(key)
    base_draw = jnp.clip(jax.random.normal(key_list[0], (TOKENS, D)), -6.0, 6.0)
    row_scale = jnp.exp(jax.random.uniform(key_list[2], (TOKENS, 1), minval=math.log(0.5), maxval=math.log(2.0)))
    marked = jnp.zeros((TOKENS,), jnp.int32).at[jnp.concatenate([first_tok, second_tok, head_tok])].set(1)
    row_scale = jnp.where(marked[:, None] == 1, 1.0, row_scale)
    return base_draw * row_scale


def draw_hidden(key, part):
    return hidden_rows(key).astype(jnp.bfloat16)


def draw_head_weight(key, part):
    key_list = jax.random.split(jax.random.fold_in(key, 505), 2)
    columns = jnp.arange(HEAD, dtype=jnp.float32) / HEAD
    base_draw = jnp.clip(jax.random.normal(key_list[0], (D, HEAD)), -6.0, 6.0)
    col_power = 0.5 * columns + 0.5 * jax.random.uniform(key_list[1], (HEAD,))
    weight = base_draw * jnp.power(10.0, col_power)[None, :] / math.sqrt(D)
    return weight.astype(jnp.bfloat16)


def tail_proj(key, which, proj_width):
    base_key = jax.random.fold_in(key, 606 + which)
    base_draw = jnp.clip(jax.random.normal(base_key, (OWNERS, D, proj_width)), -6.0, 6.0)
    return base_draw / math.sqrt(D)


def tail_out(key, which, proj_width, word_count):
    key_list = jax.random.split(jax.random.fold_in(key, 707 + which), 2)
    columns = jnp.arange(word_count, dtype=jnp.float32) / word_count
    base_draw = jnp.clip(jax.random.normal(key_list[0], (OWNERS, proj_width, word_count)), -6.0, 6.0)
    col_power = 0.5 * columns + 0.5 * jax.random.uniform(key_list[1], (OWNERS, 1, word_count))
    weight = base_draw * jnp.power(10.0, col_power) / math.sqrt(proj_width)
    return weight


def draw_tail1_proj(key, part):
    return tail_proj(key, 0, P1).astype(jnp.bfloat16)


def draw_tail2_proj(key, part):
    return tail_proj(key, 1, P2).astype(jnp.bfloat16)


def draw_tail1_out(key, part):
    return tail_out(key, 0, P1, W1).astype(jnp.bfloat16)


def draw_tail2_out(key, part):
    return tail_out(key, 1, P2, W2).astype(jnp.bfloat16)


def draw_cluster_id(key, part):
    return routing(key)[0]


def draw_target(key, part):
    cluster = routing(key)[0]
    key_list = jax.random.split(jax.random.fold_in(key, 202), 3)
    head_word = jax.random.randint(key_list[0], (TOKENS,), 0, HEAD)
    first_word = jax.random.randint(key_list[1], (TOKENS,), 0, W1)
    second_word = jax.random.randint(key_list[2], (TOKENS,), 0, W2)
    words = jnp.where(cluster < 0, head_word, jnp.where(cluster % 2 == 0, first_word, second_word)).astype(jnp.int32)
    first_head = jnp.argmax((cluster < 0).astype(jnp.int32)).astype(jnp.int32)
    return words.at[first_head].set(HEAD - 1).astype(jnp.int32)


def shard_levels(own_key, dims, cuts, low, high):
    loudness, own = 1.0, jax.random.fold_in(own_key, 6)
    for axis_at, blocks in cuts:
        draws = jnp.exp(jax.random.uniform(jax.random.fold_in(own, axis_at), (blocks,), jnp.float32, low / len(cuts), high / len(cuts)))
        loudness = loudness * jnp.repeat(draws, dims[axis_at] // blocks).reshape([-1 if axis == axis_at else 1 for axis in range(len(dims))])
    return loudness


def scatter_about(key, dims, scale, reach, cuts=(), kind=jnp.bfloat16):
    entries = jax.random.normal(key, dims, jnp.float32) * scale
    if len(cuts) > 0:
        entries = shard_levels(key, dims, cuts, -0.22, 0.18) * entries
    return jnp.clip(entries, min=-reach, max=reach).astype(kind)


def setup_inputs(seed: int = 0) -> dict:
    arg_keys = jax.random.split(jax.random.key(seed), 12)
    hidden = draw_hidden(jax.random.fold_in(arg_keys[11], 71), 0)
    pre_gates = scatter_about(arg_keys[1], (2, TOKENS, D), 1.0, 6.0, ((1, 64), (2, 8)))
    conv_weight = scatter_about(arg_keys[2], (2, K, D, D), (K * D) ** -0.5, 0.09375, ((2, 64), (3, 8)))
    head_weight = draw_head_weight(jax.random.fold_in(arg_keys[11], 71), 0)
    cluster_weight = scatter_about(arg_keys[4], (D, CLUST), 0.1, 0.59765625, ((0, 64), (1, 8)))
    tail1_proj = draw_tail1_proj(jax.random.fold_in(arg_keys[11], 71), 0)
    tail2_proj = draw_tail2_proj(jax.random.fold_in(arg_keys[11], 71), 0)
    tail1_out = draw_tail1_out(jax.random.fold_in(arg_keys[11], 71), 0)
    tail2_out = draw_tail2_out(jax.random.fold_in(arg_keys[11], 71), 0)
    cluster_id = draw_cluster_id(jax.random.fold_in(arg_keys[11], 71), 0)
    target = draw_target(jax.random.fold_in(arg_keys[11], 71), 0)
    return {"hidden": hidden, "pre_gates": pre_gates, "conv_weight": conv_weight, "head_weight": head_weight, "cluster_weight": cluster_weight, "tail1_proj": tail1_proj, "tail2_proj": tail2_proj, "tail1_out": tail1_out, "tail2_out": tail2_out, "cluster_id": cluster_id, "target": target}


def rounded(values):
    return lax.optimization_barrier(values.astype(jnp.bfloat16))


def merge_groups(row_max, row_sum, row_value):
    merged_max = jnp.max(row_max, axis=1)
    factor = jnp.exp(row_max - merged_max[:, None])
    merged_sum = jnp.sum(row_sum * factor, axis=1)
    merged_value = jnp.sum(row_value * factor[:, :, None], axis=1)
    return merged_max + jnp.log(merged_sum), merged_value / merged_sum[:, None]


def head_block(row_block, word_ids, cluster_ids, head_weight, cluster_weight, grouped_weight):
    row_count = row_block.shape[0]
    word_logits = jnp.dot(row_block, head_weight, preferred_element_type=jnp.float32).reshape(row_count, N_CH, -1)
    cluster_logits = jnp.dot(row_block, cluster_weight, preferred_element_type=jnp.float32).reshape(row_count, N_CH, -1)
    logits = jnp.concatenate([word_logits, cluster_logits], axis=2)
    row_max = jnp.max(logits, axis=2)
    expo_terms = jnp.exp(logits - row_max[:, :, None])
    row_sum = jnp.sum(expo_terms, axis=2)
    weights = rounded(expo_terms).astype(jnp.float32)
    row_value = jnp.einsum("bgj,dgj->bgd", weights, grouped_weight)
    log_total, mean_value = merge_groups(row_max, row_sum, row_value)
    head_words = HEAD // N_CH
    group_size = CLUST // N_CH
    is_tail = cluster_ids >= 0
    safe_cluster = jnp.maximum(cluster_ids, 0)
    group_index = jnp.where(is_tail, safe_cluster // group_size, word_ids // head_words).astype(jnp.int32)
    inner_index = jnp.where(is_tail, head_words + safe_cluster % group_size, word_ids % head_words).astype(jnp.int32)
    picked = logits[jnp.arange(row_count, dtype=jnp.int32), group_index, inner_index]
    column_value = grouped_weight[:, group_index, inner_index].T
    return log_total - picked, mean_value - column_value


def tier_terms(rows, word_ids, member, proj, out):
    features = rounded(jnp.dot(rows, proj, preferred_element_type=jnp.float32))
    logits = jnp.dot(features, out, preferred_element_type=jnp.float32)
    row_count = logits.shape[0]
    grouped = logits.reshape(row_count, N_CH, -1)
    row_max = jnp.max(grouped, axis=2)
    expo_terms = jnp.exp(grouped - row_max[:, :, None])
    row_sum = jnp.sum(expo_terms, axis=2)
    weights = rounded(expo_terms).astype(jnp.float32)
    out_grouped = out.reshape(out.shape[0], N_CH, -1).astype(jnp.float32)
    row_value = jnp.einsum("sgj,pgj->sgp", weights, out_grouped)
    log_total, mean_value = merge_groups(row_max, row_sum, row_value)
    column = jnp.clip(word_ids, 0, out.shape[1] - 1).astype(jnp.int32)
    picked = jnp.take_along_axis(logits, column[:, None], axis=1)[:, 0]
    column_value = jnp.take(out, column, axis=1).T.astype(jnp.float32)
    tail_dz = rounded(jnp.where(member[:, None], mean_value - column_value, 0.0))
    probability = jnp.exp(logits - log_total[:, None])
    positions = jnp.arange(out.shape[1], dtype=jnp.int32)
    target_hot = (positions[None, :] == column[:, None]).astype(jnp.float32)
    dlogit = rounded(jnp.where(member[:, None], probability - target_hot, 0.0))
    out_grad = jnp.einsum("sp,sw->pw", features.astype(jnp.float32), dlogit.astype(jnp.float32))
    proj_grad = jnp.einsum("sd,sp->dp", rows.astype(jnp.float32), tail_dz.astype(jnp.float32))
    returned = jnp.einsum("sp,dp->sd", tail_dz.astype(jnp.float32), proj.astype(jnp.float32))
    tail_loss = jnp.where(member, log_total - picked, 0.0)
    return out_grad, proj_grad, returned, tail_loss


def reference(hidden, pre_gates, conv_weight, head_weight, cluster_weight, tail1_proj, tail2_proj, tail1_out, tail2_out, cluster_id, target):
    grouped_weight = jnp.concatenate([head_weight.reshape(D, N_CH, -1), cluster_weight.reshape(D, N_CH, -1)], axis=2).astype(jnp.float32)

    def head_step(pieces):
        return head_block(pieces[0], pieces[1], pieces[2], head_weight, cluster_weight, grouped_weight)

    head_loss, head_grad = lax.map(head_step, (hidden.reshape(N_TOK, TOK_DEV, D), target.reshape(N_TOK, TOK_DEV), cluster_id.reshape(N_TOK, TOK_DEV)))
    head_loss = head_loss.reshape(TOKENS)
    head_grad = head_grad.reshape(TOKENS, D)

    tokens_all = jnp.arange(TOKENS, dtype=jnp.int32)
    is_tail = cluster_id >= 0
    owner_ids = jnp.where(is_tail, cluster_id // 2, 0).astype(jnp.int32)
    tier_ids = jnp.where(is_tail, cluster_id % 2, -1).astype(jnp.int32)
    source = tokens_all // TOK_DEV
    owner_range = jnp.arange(OWNERS, dtype=jnp.int32)
    hits = ((owner_ids.reshape(N_TOK, TOK_DEV, 1) == owner_range[None, None, :]) & is_tail.reshape(N_TOK, TOK_DEV, 1)).astype(jnp.int32)
    running = jnp.cumsum(hits, axis=1)
    slot_ids = (jnp.sum(running * hits, axis=2) - 1).reshape(TOKENS).astype(jnp.int32)
    flat_index = jnp.where(is_tail, owner_ids * SLOTS + source * CAP + slot_ids, OWNERS * SLOTS).astype(jnp.int32)
    table = jnp.full((OWNERS * SLOTS + 1,), TOKENS, jnp.int32).at[flat_index].set(tokens_all)[:-1].reshape(OWNERS, SLOTS)
    hidden_pad = jnp.concatenate([hidden, jnp.zeros((1, D), jnp.bfloat16)], axis=0)
    target_pad = jnp.concatenate([target, jnp.zeros((1,), jnp.int32)], axis=0)
    tier_pad = jnp.concatenate([tier_ids, jnp.full((1,), -1, jnp.int32)], axis=0)

    def owner_step(pieces):
        index_row, first_proj, second_proj, first_out, second_out = pieces
        rows = hidden_pad[index_row]
        word_ids = target_pad[index_row]
        tiers = tier_pad[index_row]
        first = tier_terms(rows, word_ids, tiers == 0, first_proj, first_out)
        second = tier_terms(rows, word_ids, tiers == 1, second_proj, second_out)
        return first[0], second[0], first[1], second[1], first[2] + second[2], first[3] + second[3]

    out1_grad, out2_grad, proj1_grad, proj2_grad, returned, tail_loss = lax.map(owner_step, (table, tail1_proj, tail2_proj, tail1_out, tail2_out))
    table_flat = table.reshape(-1)
    tail_back = jnp.zeros((TOKENS + 1, D), jnp.float32).at[table_flat].set(returned.reshape(-1, D))[:TOKENS]
    tail_tok_loss = jnp.zeros((TOKENS + 1,), jnp.float32).at[table_flat].set(tail_loss.reshape(-1))[:TOKENS]
    token_loss = head_loss + tail_tok_loss

    grad_sum = head_grad + tail_back
    gate_a = pre_gates[0].astype(jnp.float32)
    gate_sig = jax.nn.sigmoid(pre_gates[1].astype(jnp.float32))
    grad_a = (grad_sum * gate_sig).astype(jnp.bfloat16)
    grad_b = (grad_sum * gate_a * gate_sig * (1.0 - gate_sig)).astype(jnp.bfloat16)
    total_grad = grad_sum
    for offset_rows in range(K):
        for half_index, gate_grad in ((0, grad_a), (1, grad_b)):
            blocks = gate_grad.reshape(TOKENS // LEN, LEN, D)
            shifted = jnp.pad(blocks[:, offset_rows:], ((0, 0), (0, offset_rows), (0, 0))).reshape(TOKENS, D)
            total_grad = total_grad + jnp.dot(shifted, conv_weight[half_index, offset_rows].T, preferred_element_type=jnp.float32)
    grad_input = total_grad.astype(jnp.bfloat16)
    return (token_loss, grad_input, proj1_grad, proj2_grad, out1_grad, out2_grad)
```

```python
import functools

import jax
import jax.numpy as jnp
from jax import lax
from jax.experimental import pallas as pl
from jax.experimental.pallas import tpu as pltpu
from jax.sharding import PartitionSpec as P

K = 4
LEN = 128
T = 128
D = 1024
OWN = 64
NCH = 8
NAR = 128
HW = 2560
CW = 16
GW = HW + CW
HP = 2688
BLK = 384
CONV = 2 * K * NAR
W1 = 384
W2 = 1152
P1 = 256
P2 = 64
SROW = 16
NEG = -1e30
f32 = jnp.float32
bf16 = jnp.bfloat16
VMEM = pl.BlockSpec(memory_space=pltpu.VMEM)
SMEM = pl.BlockSpec(memory_space=pltpu.SMEM)
ANY = pl.BlockSpec(memory_space=pl.ANY)


def dot(a, b, ca=1, cb=0):
    return lax.dot_general(a, b, (((ca,), (cb,)), ((), ())), preferred_element_type=f32)


def parts3(x):
    hi = x.astype(bf16).astype(f32)
    rest = x - hi
    mid = rest.astype(bf16).astype(f32)
    return [hi, mid, rest - mid]


def iota(shape, axis):
    return lax.broadcasted_iota(jnp.int32, shape, axis)


def call(kernel, outs, *args, specs=None, scratch=(), flops=10**7, nbytes=10**6):
    outs = [jax.ShapeDtypeStruct(shape, kind) for shape, kind in outs]
    return pl.pallas_call(
        kernel,
        out_shape=outs,
        in_specs=[VMEM] * len(args) if specs is None else specs,
        out_specs=[VMEM] * len(outs),
        scratch_shapes=list(scratch),
        cost_estimate=pl.CostEstimate(flops=flops, bytes_accessed=nbytes, transcendentals=0),
    )(*args)


def route_kernel(cid_row, cid_col, tgt_col, hidden, send, pick):
    owner_row = jnp.where(cid_row[...] >= 0, cid_row[...] // 2, -1)
    owner_col = jnp.where(cid_col[...] >= 0, cid_col[...] // 2, -2)
    before = (owner_col == owner_row) & (iota((T, T), 0) < iota((T, T), 1))
    rank = jnp.sum(before.astype(f32), axis=0, keepdims=True).astype(jnp.int32)
    slot = jnp.where(owner_row >= 0, owner_row * 2 + rank, -1)
    chosen = (iota((T, T), 0) == slot).astype(bf16)
    pick[...] = chosen
    send[:, :D] = dot(chosen, hidden[...]).astype(bf16)
    lane = iota((T, 128), 1)
    word = tgt_col[...]
    tier = jnp.where(cid_col[...] >= 0, cid_col[...] % 2 + 1, 0)
    meta = jnp.where(lane == 0, word // 128, jnp.where(lane == 1, word % 128, jnp.where(lane == 2, tier, 0)))
    send[:, D:] = dot(chosen, meta.astype(f32).astype(bf16)).astype(bf16)


def slot_meta(meta):
    meta = meta.astype(f32)
    word = (meta[:, 0:1] * 128.0 + meta[:, 1:2]).astype(jnp.int32)
    tier = meta[:, 2:3].astype(jnp.int32)
    return word, tier


def tail_kernel(ch, rows, meta, proj1, proj2, out1, out2, feat, part):
    word, tier = slot_meta(meta[...])
    first = tier == 1
    z1 = dot(rows[...], proj1[...])
    z2 = dot(rows[...], proj2[...])
    features = jnp.where(first, z1, z2).astype(bf16)
    feat[...] = features

    def local(out, width):
        logits = dot(features, out[...])
        top = jnp.max(logits, axis=1, keepdims=True)
        terms = jnp.exp(logits - top)
        total = jnp.sum(terms, axis=1, keepdims=True)
        hot = iota((T, width), 1) == word - ch[0] * width
        target = jnp.sum(jnp.where(hot, logits, 0.0), axis=1, keepdims=True)
        value = dot(jnp.where(hot, 0.0, terms).astype(bf16), out[...], 1, 1)
        column = dot(hot.astype(f32).astype(bf16), out[...], 1, 1)
        return top, total, target, value, column

    one = local(out1, W1)
    two = local(out2, W2)
    top, total, target, value, column = [jnp.where(first, a, b) for a, b in zip(one, two)]
    part[:, :P1] = value.astype(bf16)
    part[:, P1 : 2 * P1] = column.astype(bf16)
    lane = iota((T, 128), 1)
    stats = jnp.zeros((T, 128), f32)
    for i, x in enumerate(parts3(top) + parts3(total) + parts3(target)):
        stats = jnp.where(lane == i, x, stats)
    part[:, 2 * P1 :] = stats.astype(bf16)


def tail_merge_kernel(meta, parts, proj1_part, proj2_part, dz1, dz2, log_total, back):
    _, tier = slot_meta(meta[...])
    tops, totals, target = [], [], 0.0
    for g in range(NCH):
        stats = parts[g, :, 2 * P1 :].astype(f32)
        s3 = [stats[:, i : i + 1] for i in range(9)]
        tops.append(s3[0] + s3[1] + s3[2])
        totals.append(s3[3] + s3[4] + s3[5])
        target = target + (s3[6] + s3[7] + s3[8])
    top = functools.reduce(jnp.maximum, tops)
    scales = [jnp.exp(t - top) for t in tops]
    total = sum(s * t for s, t in zip(scales, totals))
    log_all = top + jnp.log(total)
    inverse = 1.0 / total
    value = jnp.zeros((T, P1), f32)
    column = jnp.zeros((T, P1), f32)
    for g in range(NCH):
        value = value + parts[g, :, :P1].astype(f32) * (scales[g] * inverse)
        column = column + parts[g, :, P1 : 2 * P1].astype(f32)
    dz = value + (jnp.exp(target - log_all) - 1.0) * column
    one = jnp.where(tier == 1, dz, 0.0).astype(bf16)
    two = jnp.where(tier == 2, dz, 0.0).astype(bf16)
    dz1[...] = one
    dz2[...] = two
    log_total[...] = jnp.broadcast_to(log_all, (T, 128))
    back[:, :NAR] = (dot(one, proj1_part[...], 1, 1) + dot(two, proj2_part[...], 1, 1)).astype(bf16)
    loss = jnp.where(tier > 0, log_all - target, 0.0)
    lane = iota((T, 128), 1)
    tail = jnp.zeros((T, 128), f32)
    for i, x in enumerate(parts3(loss)):
        tail = jnp.where(lane == i, x, tail)
    back[:, NAR:] = tail.astype(bf16)


def tail_grad_kernel(ch, meta, feat, rows_part, dz1, dz2, log_total, out1, out2, g_out1, g_out2, g_proj1, g_proj2):
    word, tier = slot_meta(meta[...])
    features = feat[...]
    log_all = log_total[:, 0:1]

    def slope(out, width, which):
        logits = dot(features, out[...])
        hot = (iota((T, width), 1) == word - ch[0] * width).astype(f32)
        return jnp.where(tier == which, jnp.exp(logits - log_all) - hot, 0.0).astype(bf16)

    g_out1[...] = dot(features, slope(out1, W1, 1), 0, 0)
    g_out2[...] = dot(features, slope(out2, W2, 2), 0, 0)[:P2]
    g_proj1[...] = dot(rows_part[...], dz1[...], 0, 0)
    g_proj2[...] = dot(rows_part[...], dz2[...], 0, 0)[:, :P2]


def back_kernel(got, pick, back_t, loss):
    back_t[...] = dot(got[:, :NAR], pick[...], 0, 0)
    terms = dot(got[:, NAR:], pick[...], 0, 0)
    loss[...] = terms[0:1] + terms[1:2] + terms[2:3]


def head_kernel(col, hidden, weight, out, acc, stat):
    step = pl.program_id(0)

    @pl.when(step == 0)
    def _():
        acc[...] = jnp.zeros_like(acc)
        stat[0:1, :] = jnp.full((1, T), NEG, f32)
        stat[1:2, :] = jnp.zeros((1, T), f32)
        stat[2:3, :] = jnp.zeros((1, T), f32)

    logits = dot(hidden[...], weight[...]).T
    index = iota((BLK, T), 0) + step * BLK
    logits = jnp.where(index < GW, logits, NEG)
    old = stat[0:1, :]
    top = jnp.maximum(old, jnp.max(logits, axis=0, keepdims=True))
    scale = jnp.exp(old - top)
    terms = jnp.exp(logits - top)
    hot = index == col[...]
    stat[0:1, :] = top
    stat[1:2, :] = stat[1:2, :] * scale + jnp.sum(terms, axis=0, keepdims=True)
    stat[2:3, :] = stat[2:3, :] + jnp.sum(jnp.where(hot, logits, 0.0), axis=0, keepdims=True)
    right = jnp.concatenate([jnp.where(hot, 0.0, terms), hot.astype(f32)], axis=1).astype(bf16)
    new = dot(weight[...], right)
    acc[:, :T] = acc[:, :T] * scale + new[:, :T]
    acc[:, T:] = acc[:, T:] + new[:, T:]

    @pl.when(step == pl.num_programs(0) - 1)
    def _():
        line = iota((SROW, 2 * T), 0)
        stats = jnp.zeros((SROW, 2 * T), f32)
        rows = parts3(stat[0:1, :]) + parts3(stat[1:2, :]) + parts3(stat[2:3, :])
        for i, x in enumerate(rows):
            stats = jnp.where(line == i, jnp.concatenate([x, x], axis=1), stats)
        for g in range(NCH):
            out[g, :NAR, :] = acc[g * NAR : (g + 1) * NAR, :].astype(bf16)
            out[g, NAR:, :] = stats.astype(bf16)


def head_call(col, hidden, weight):
    return pl.pallas_call(
        head_kernel,
        out_shape=jax.ShapeDtypeStruct((NCH, NAR + SROW, 2 * T), bf16),
        grid=(HP // BLK,),
        in_specs=[
            pl.BlockSpec((1, T), lambda i: (0, 0)),
            pl.BlockSpec((T, D), lambda i: (0, 0)),
            pl.BlockSpec((D, BLK), lambda i: (0, i)),
        ],
        out_specs=pl.BlockSpec((NCH, NAR + SROW, 2 * T), lambda i: (0, 0, 0)),
        scratch_shapes=[pltpu.VMEM((D, 2 * T), f32), pltpu.VMEM((8, T), f32)],
        compiler_params=pltpu.CompilerParams(dimension_semantics=("arbitrary",)),
        cost_estimate=pl.CostEstimate(flops=2 * 10**9, bytes_accessed=6 * 10**6, transcendentals=0),
    )(col, hidden, weight)


def conv_kernel(parts, back_t, tail_loss, gates, weight, conv, grad, loss, taps, wide, sem):
    copy = pltpu.make_async_copy(weight.at[:, pl.ds(HP, CONV)], wide, sem)
    copy.start()
    tops, totals, target = [], [], 0.0
    for g in range(NCH):
        stats = parts[g, NAR:, :T].astype(f32)
        s3 = [stats[i : i + 1] for i in range(9)]
        tops.append(s3[0] + s3[1] + s3[2])
        totals.append(s3[3] + s3[4] + s3[5])
        target = target + (s3[6] + s3[7] + s3[8])
    top = functools.reduce(jnp.maximum, tops)
    scales = [jnp.exp(t - top) for t in tops]
    total = sum(s * t for s, t in zip(scales, totals))
    log_all = top + jnp.log(total)
    inverse = 1.0 / total
    loss[...] = log_all - target + tail_loss[...]
    dh = back_t[...]
    column = jnp.zeros((NAR, T), f32)
    for g in range(NCH):
        dh = dh + parts[g, :NAR, :T].astype(f32) * (scales[g] * inverse)
        column = column + parts[g, :NAR, T:].astype(f32)
    dh = dh + (jnp.exp(target - log_all) - 1.0) * column
    grad[...] = dh
    a = gates[0].astype(f32)
    sig = 1.0 / (1.0 + jnp.exp(-gates[1].astype(f32)))
    da = dh * sig
    db = da * a * (1.0 - sig)
    lane = iota((NAR, T), 1)
    for half, value in enumerate((da, db)):
        for k in range(K):
            moved = value if k == 0 else jnp.where(lane < T - k, pltpu.roll(value, T - k, 1), 0.0)
            at = (half * K + k) * NAR
            taps[at : at + NAR, :] = moved.astype(bf16)
    copy.wait()
    total_conv = dot(wide[...], taps[...])
    for g in range(NCH):
        conv[g] = total_conv[g * NAR : (g + 1) * NAR].astype(bf16)


def final_kernel(parts, grad, out):
    total = grad[...]
    for g in range(NCH):
        total = total + parts[g].astype(f32)
    out[...] = total.T.astype(bf16)


def on_device(hidden, pre_gates, conv_weight, head_weight, cluster_weight, tail1_proj, tail2_proj, tail1_out, tail2_out, cluster_id, target):
    ch = lax.axis_index("ch").astype(jnp.int32)
    ch_arr = ch.reshape(1)
    packed = jnp.concatenate(
        [
            head_weight,
            cluster_weight,
            jnp.zeros((head_weight.shape[0], HP - GW), bf16),
            conv_weight.transpose(2, 0, 1, 3).reshape(head_weight.shape[0], CONV),
        ],
        axis=1,
    )
    gathered = lax.all_gather(packed, "tok", axis=0, tiled=True)

    send, pick = call(
        route_kernel,
        [((T, D + 128), bf16), ((T, T), bf16)],
        cluster_id.reshape(1, T),
        cluster_id.reshape(T, 1),
        target.reshape(T, 1),
        hidden,
    )
    got = lax.all_to_all(send.reshape(OWN, 2, D + 128), "tok", split_axis=0, concat_axis=0, tiled=True).reshape(T, D + 128)
    rows, meta = got[:, :D], got[:, D:]
    proj1 = tail1_proj[0]
    proj2 = jnp.pad(tail2_proj[0], ((0, 0), (0, P1 - P2)))
    out1 = tail1_out[0]
    out2 = jnp.pad(tail2_out[0], ((0, P1 - P2), (0, 0)))
    col_start = ch * NAR
    proj1_part = lax.dynamic_slice_in_dim(proj1, col_start, NAR, 0)
    proj2_part = lax.dynamic_slice_in_dim(proj2, col_start, NAR, 0)
    rows_part = lax.dynamic_slice_in_dim(rows, col_start, NAR, 1)
    feat, part = call(
        tail_kernel,
        [((T, P1), bf16), ((T, 2 * P1 + 128), bf16)],
        ch_arr, rows, meta, proj1, proj2, out1, out2,
        specs=[SMEM] + [VMEM] * 6,
    )
    parts = lax.all_to_all(
        jnp.broadcast_to(part[None], (NCH,) + part.shape), "ch", split_axis=0, concat_axis=0, tiled=True
    )
    dz1, dz2, log_total, back = call(
        tail_merge_kernel,
        [((T, P1), bf16), ((T, P1), bf16), ((T, 128), f32), ((T, NAR + 128), bf16)],
        meta, parts, proj1_part, proj2_part,
    )
    got_back = lax.all_to_all(back.reshape(OWN, 2, NAR + 128), "tok", split_axis=0, concat_axis=0, tiled=True).reshape(T, NAR + 128)
    g_out1, g_out2, g_proj1, g_proj2 = call(
        tail_grad_kernel,
        [((P1, W1), f32), ((P2, W2), f32), ((NAR, P1), f32), ((NAR, P2), f32)],
        ch_arr, meta, feat, rows_part, dz1, dz2, log_total, out1, out2,
        specs=[SMEM] + [VMEM] * 8,
    )
    back_t, tail_loss = call(back_kernel, [((NAR, T), f32), ((1, T), f32)], got_back, pick)

    is_tail = cluster_id >= 0
    word_local = target - ch * HW
    cluster_local = cluster_id - ch * CW
    local = jnp.where(
        is_tail,
        jnp.where((cluster_local >= 0) & (cluster_local < CW), HW + cluster_local, -1),
        jnp.where((word_local >= 0) & (word_local < HW), word_local, -1),
    )
    gathered, back_t = lax.optimization_barrier((gathered, back_t))
    head = head_call(local.reshape(1, T), hidden, gathered)
    head_parts = lax.all_to_all(head, "ch", split_axis=0, concat_axis=0, tiled=True)
    conv, grad, loss = call(
        conv_kernel,
        [((NCH, NAR, T), bf16), ((NAR, T), f32), ((1, T), f32)],
        head_parts, back_t, tail_loss, pre_gates.transpose(0, 2, 1), gathered,
        specs=[VMEM] * 4 + [ANY],
        scratch=[pltpu.VMEM((CONV, T), bf16), pltpu.VMEM((D, CONV), bf16), pltpu.SemaphoreType.DMA],
    )
    conv_parts = lax.all_to_all(conv, "ch", split_axis=0, concat_axis=0, tiled=True)
    (grad_input,) = call(final_kernel, [((T, NAR), bf16)], conv_parts, grad)
    return (loss.reshape(T), grad_input, g_proj1[None], g_proj2[None], g_out1[None], g_out2[None])


def solution(mesh):
    placed = (
        P("tok", None),
        P(None, "tok", "ch"),
        P(None, None, "tok", "ch"),
        P("tok", "ch"),
        P("tok", "ch"),
        P("tok", None, None),
        P("tok", None, None),
        P("tok", None, "ch"),
        P("tok", None, "ch"),
        P("tok"),
        P("tok"),
    )
    return jax.shard_map(
        on_device,
        mesh=mesh,
        in_specs=placed,
        out_specs=(
            P("tok"),
            P("tok", "ch"),
            P("tok", "ch", None),
            P("tok", "ch", None),
            P("tok", None, "ch"),
            P("tok", None, "ch"),
        ),
        check_vma=False,
    )
```

```python
import functools

import jax
import jax.numpy as jnp
from jax import lax
from jax.experimental import pallas as pl
from jax.experimental.pallas import tpu as pltpu
from jax.sharding import PartitionSpec as P

K = 4
LEN = 128
T = 128
D = 1024
OWN = 64
NCH = 8
NAR = 128
HW = 2560
CW = 16
GW = HW + CW
HP = 2688
BLK = 896
CONV = 2 * K * NAR
W1 = 384
W2 = 1152
P1 = 256
P2 = 64
SROW = 16
NEG = -1e30
LIMIT = 24 * 2**20
f32 = jnp.float32
bf16 = jnp.bfloat16
VMEM = pl.BlockSpec(memory_space=pltpu.VMEM)
SMEM = pl.BlockSpec(memory_space=pltpu.SMEM)


def dot(a, b, ca=1, cb=0):
    return lax.dot_general(a, b, (((ca,), (cb,)), ((), ())), preferred_element_type=f32)


def parts3(x):
    hi = x.astype(bf16).astype(f32)
    rest = x - hi
    mid = rest.astype(bf16).astype(f32)
    return [hi, mid, rest - mid]


def iota(shape, axis):
    return lax.broadcasted_iota(jnp.int32, shape, axis)


def call(kernel, outs, *args, specs=None, scratch=(), limit=None, flops=10**7, nbytes=10**6):
    outs = [jax.ShapeDtypeStruct(shape, kind) for shape, kind in outs]
    return pl.pallas_call(
        kernel,
        out_shape=outs,
        in_specs=[VMEM] * len(args) if specs is None else specs,
        out_specs=[VMEM] * len(outs),
        scratch_shapes=list(scratch),
        compiler_params=pltpu.CompilerParams(vmem_limit_bytes=limit),
        cost_estimate=pl.CostEstimate(flops=flops, bytes_accessed=nbytes, transcendentals=0),
    )(*args)


def pack_kernel(head, cluster, conv, out):
    out[:, :HW] = head[...]
    out[:, HW:HP] = jnp.zeros((out.shape[0], HP - HW), bf16)
    out[:, HW:GW] = cluster[...]
    for half in range(2):
        for k in range(K):
            at = HP + (half * K + k) * NAR
            out[:, at : at + NAR] = conv[half, k]


def route_kernel(cid, tgt, hidden, send, pick):
    cid_row = jnp.broadcast_to(cid[...], (T, T))
    cid_col = cid_row.astype(f32).T.astype(jnp.int32)
    word = jnp.broadcast_to(tgt[...], (T, T)).astype(f32).T.astype(jnp.int32)
    owner_row = jnp.where(cid_row >= 0, cid_row // 2, -1)
    owner_col = jnp.where(cid_col >= 0, cid_col // 2, -2)
    before = (owner_col == owner_row) & (iota((T, T), 0) < iota((T, T), 1))
    rank = jnp.sum(before.astype(f32), axis=0, keepdims=True).astype(jnp.int32)
    slot = jnp.where(owner_row >= 0, owner_row * 2 + rank, -1)
    chosen = (iota((T, T), 0) == slot).astype(bf16)
    pick[...] = chosen
    send[:, :D] = dot(chosen, hidden[...]).astype(bf16)
    lane = iota((T, T), 1)
    tier = jnp.where(cid_col >= 0, cid_col % 2 + 1, 0)
    meta = jnp.where(lane == 0, word // 128, jnp.where(lane == 1, word % 128, jnp.where(lane == 2, tier, 0)))
    send[:, D:] = dot(chosen, meta.astype(f32).astype(bf16)).astype(bf16)


def slot_meta(meta):
    meta = meta.astype(f32)
    word = (meta[:, 0:1] * 128.0 + meta[:, 1:2]).astype(jnp.int32)
    tier = meta[:, 2:3].astype(jnp.int32)
    return word, tier


def tail_kernel(ch, got, proj1, proj2, out1, out2, feat, part):
    word, tier = slot_meta(got[:, D:])
    rows = got[:, :D]
    first = tier == 1
    z1 = dot(rows, proj1[...])
    z2 = dot(rows, proj2[...])
    features = jnp.where(first, z1, z2).astype(bf16)
    feat[...] = features

    def local(out, width):
        logits = dot(features, out[...])
        top = jnp.max(logits, axis=1, keepdims=True)
        terms = jnp.exp(logits - top)
        total = jnp.sum(terms, axis=1, keepdims=True)
        hot = iota((T, width), 1) == word - ch[0] * width
        target = jnp.sum(jnp.where(hot, logits, 0.0), axis=1, keepdims=True)
        value = dot(jnp.where(hot, 0.0, terms).astype(bf16), out[...], 1, 1)
        column = dot(hot.astype(f32).astype(bf16), out[...], 1, 1)
        return top, total, target, value, column

    one = local(out1, W1)
    two = local(out2, W2)
    top, total, target, value, column = [jnp.where(first, a, b) for a, b in zip(one, two)]
    value = value.astype(bf16)
    column = column.astype(bf16)
    lane = iota((T, 128), 1)
    stats = jnp.zeros((T, 128), f32)
    for i, x in enumerate(parts3(top) + parts3(total) + parts3(target)):
        stats = jnp.where(lane == i, x, stats)
    stats = stats.astype(bf16)
    for g in range(NCH):
        part[g, :, :P1] = value
        part[g, :, P1 : 2 * P1] = column
        part[g, :, 2 * P1 :] = stats


def tail_merge_kernel(ch, got, parts, proj1, proj2, dz1, dz2, log_total, back):
    _, tier = slot_meta(got[:, D:])
    tops, totals, target = [], [], 0.0
    for g in range(NCH):
        stats = parts[g, :, 2 * P1 :].astype(f32)
        s3 = [stats[:, i : i + 1] for i in range(9)]
        tops.append(s3[0] + s3[1] + s3[2])
        totals.append(s3[3] + s3[4] + s3[5])
        target = target + (s3[6] + s3[7] + s3[8])
    top = functools.reduce(jnp.maximum, tops)
    scales = [jnp.exp(t - top) for t in tops]
    total = sum(s * t for s, t in zip(scales, totals))
    log_all = top + jnp.log(total)
    inverse = 1.0 / total
    value = jnp.zeros((T, P1), f32)
    column = jnp.zeros((T, P1), f32)
    for g in range(NCH):
        value = value + parts[g, :, :P1].astype(f32) * (scales[g] * inverse)
        column = column + parts[g, :, P1 : 2 * P1].astype(f32)
    dz = value + (jnp.exp(target - log_all) - 1.0) * column
    one = jnp.where(tier == 1, dz, 0.0).astype(bf16)
    two = jnp.where(tier == 2, dz, 0.0).astype(bf16)
    dz1[...] = one
    dz2[...] = two
    log_total[...] = jnp.broadcast_to(log_all, (T, 128))
    mine = pl.ds(pl.multiple_of(ch[0] * NAR, NAR), NAR)
    back[:, :NAR] = (dot(one, proj1[mine, :], 1, 1) + dot(two, proj2[mine, :], 1, 1)).astype(bf16)
    loss = jnp.where(tier > 0, log_all - target, 0.0)
    lane = iota((T, 128), 1)
    tail = jnp.zeros((T, 128), f32)
    for i, x in enumerate(parts3(loss)):
        tail = jnp.where(lane == i, x, tail)
    back[:, NAR:] = tail.astype(bf16)


def tail_grad_kernel(ch, got, feat, dz1, dz2, log_total, out1, out2, g_out1, g_out2, g_proj1, g_proj2):
    word, tier = slot_meta(got[:, D:])
    rows_part = got[:, pl.ds(pl.multiple_of(ch[0] * NAR, NAR), NAR)]
    features = feat[...]
    log_all = log_total[:, 0:1]

    def slope(out, width, which):
        logits = dot(features, out[...])
        hot = (iota((T, width), 1) == word - ch[0] * width).astype(f32)
        return jnp.where(tier == which, jnp.exp(logits - log_all) - hot, 0.0).astype(bf16)

    g_out1[...] = dot(features, slope(out1, W1, 1), 0, 0)
    g_out2[...] = dot(features, slope(out2, W2, 2), 0, 0)[:P2]
    g_proj1[...] = dot(rows_part, dz1[...], 0, 0)
    g_proj2[...] = dot(rows_part, dz2[...], 0, 0)[:, :P2]


def back_kernel(got, pick, back_t, loss):
    back_t[...] = dot(got[:, :NAR], pick[...], 0, 0)
    terms = dot(got[:, NAR:], pick[...], 0, 0)
    loss[...] = terms[0:1] + terms[1:2] + terms[2:3]


def head_kernel(col, hidden, weight, out, acc, stat):
    step = pl.program_id(0)

    @pl.when(step == 0)
    def _():
        acc[...] = jnp.zeros_like(acc)
        stat[0:1, :] = jnp.full((1, T), NEG, f32)
        stat[1:2, :] = jnp.zeros((1, T), f32)
        stat[2:3, :] = jnp.zeros((1, T), f32)

    logits = dot(hidden[...], weight[...]).T
    index = iota((BLK, T), 0) + step * BLK
    logits = jnp.where(index < GW, logits, NEG)
    old = stat[0:1, :]
    top = jnp.maximum(old, jnp.max(logits, axis=0, keepdims=True))
    scale = jnp.exp(old - top)
    terms = jnp.exp(logits - top)
    hot = index == col[...]
    stat[0:1, :] = top
    stat[1:2, :] = stat[1:2, :] * scale + jnp.sum(terms, axis=0, keepdims=True)
    stat[2:3, :] = stat[2:3, :] + jnp.sum(jnp.where(hot, logits, 0.0), axis=0, keepdims=True)
    right = jnp.concatenate([jnp.where(hot, 0.0, terms), hot.astype(f32)], axis=1).astype(bf16)
    new = dot(weight[...], right)
    acc[:, :T] = acc[:, :T] * scale + new[:, :T]
    acc[:, T:] = acc[:, T:] + new[:, T:]

    @pl.when(step == pl.num_programs(0) - 1)
    def _():
        line = iota((SROW, 2 * T), 0)
        stats = jnp.zeros((SROW, 2 * T), f32)
        rows = parts3(stat[0:1, :]) + parts3(stat[1:2, :]) + parts3(stat[2:3, :])
        for i, x in enumerate(rows):
            stats = jnp.where(line == i, jnp.concatenate([x, x], axis=1), stats)
        for g in range(NCH):
            out[g, :NAR, :] = acc[g * NAR : (g + 1) * NAR, :].astype(bf16)
            out[g, NAR:, :] = stats.astype(bf16)


def head_call(col, hidden, weight):
    return pl.pallas_call(
        head_kernel,
        out_shape=jax.ShapeDtypeStruct((NCH, NAR + SROW, 2 * T), bf16),
        grid=(HP // BLK,),
        in_specs=[
            pl.BlockSpec((1, T), lambda i: (0, 0)),
            pl.BlockSpec((T, D), lambda i: (0, 0)),
            pl.BlockSpec((D, BLK), lambda i: (0, i)),
        ],
        out_specs=pl.BlockSpec((NCH, NAR + SROW, 2 * T), lambda i: (0, 0, 0)),
        scratch_shapes=[pltpu.VMEM((D, 2 * T), f32), pltpu.VMEM((8, T), f32)],
        compiler_params=pltpu.CompilerParams(dimension_semantics=("arbitrary",)),
        cost_estimate=pl.CostEstimate(flops=2 * 10**9, bytes_accessed=6 * 10**6, transcendentals=0),
    )(col, hidden, weight)


def conv_kernel(parts, back_t, tail_loss, gates, weight, conv, grad, loss, taps):
    tops, totals, target = [], [], 0.0
    for g in range(NCH):
        stats = parts[g, NAR:, :T].astype(f32)
        s3 = [stats[i : i + 1] for i in range(9)]
        tops.append(s3[0] + s3[1] + s3[2])
        totals.append(s3[3] + s3[4] + s3[5])
        target = target + (s3[6] + s3[7] + s3[8])
    top = functools.reduce(jnp.maximum, tops)
    scales = [jnp.exp(t - top) for t in tops]
    total = sum(s * t for s, t in zip(scales, totals))
    log_all = top + jnp.log(total)
    inverse = 1.0 / total
    loss[...] = log_all - target + tail_loss[...]
    dh = back_t[...]
    column = jnp.zeros((NAR, T), f32)
    for g in range(NCH):
        dh = dh + parts[g, :NAR, :T].astype(f32) * (scales[g] * inverse)
        column = column + parts[g, :NAR, T:].astype(f32)
    dh = dh + (jnp.exp(target - log_all) - 1.0) * column
    grad[...] = dh
    a = gates[0].astype(f32)
    sig = 1.0 / (1.0 + jnp.exp(-gates[1].astype(f32)))
    da = dh * sig
    db = da * a * (1.0 - sig)
    lane = iota((NAR, T), 1)
    for half, value in enumerate((da, db)):
        for k in range(K):
            moved = value if k == 0 else jnp.where(lane < T - k, pltpu.roll(value, T - k, 1), 0.0)
            at = (half * K + k) * NAR
            taps[at : at + NAR, :] = moved.astype(bf16)
    total_conv = dot(weight[...], taps[...])
    for g in range(NCH):
        conv[g] = total_conv[g * NAR : (g + 1) * NAR].astype(bf16)


def final_kernel(parts, grad, out):
    total = grad[...]
    for g in range(NCH):
        total = total + parts[g].astype(f32)
    out[...] = total.T.astype(bf16)


def on_device(hidden, pre_gates, conv_weight, head_weight, cluster_weight, tail1_proj, tail2_proj, tail1_out, tail2_out, cluster_id, target):
    ch = lax.axis_index("ch").astype(jnp.int32)
    ch_arr = ch.reshape(1)
    (packed,) = call(pack_kernel, [((head_weight.shape[0], HP + CONV), bf16)], head_weight, cluster_weight, conv_weight)
    gathered = lax.all_gather(packed, "tok", axis=0, tiled=True)

    send, pick = call(
        route_kernel,
        [((T, D + 128), bf16), ((T, T), bf16)],
        cluster_id.reshape(1, T),
        target.reshape(1, T),
        hidden,
    )
    got = lax.all_to_all(send.reshape(OWN, 2, D + 128), "tok", split_axis=0, concat_axis=0, tiled=True).reshape(T, D + 128)
    proj1 = tail1_proj[0]
    proj2 = jnp.pad(tail2_proj[0], ((0, 0), (0, P1 - P2)))
    out1 = tail1_out[0]
    out2 = jnp.pad(tail2_out[0], ((0, P1 - P2), (0, 0)))
    feat, part = call(
        tail_kernel,
        [((T, P1), bf16), ((NCH, T, 2 * P1 + 128), bf16)],
        ch_arr, got, proj1, proj2, out1, out2,
        specs=[SMEM] + [VMEM] * 5,
    )
    parts = lax.all_to_all(part, "ch", split_axis=0, concat_axis=0, tiled=True)
    dz1, dz2, log_total, back = call(
        tail_merge_kernel,
        [((T, P1), bf16), ((T, P1), bf16), ((T, 128), f32), ((T, NAR + 128), bf16)],
        ch_arr, got, parts, proj1, proj2,
        specs=[SMEM] + [VMEM] * 4,
    )
    got_back = lax.all_to_all(back.reshape(OWN, 2, NAR + 128), "tok", split_axis=0, concat_axis=0, tiled=True).reshape(T, NAR + 128)
    g_out1, g_out2, g_proj1, g_proj2 = call(
        tail_grad_kernel,
        [((P1, W1), f32), ((P2, W2), f32), ((NAR, P1), f32), ((NAR, P2), f32)],
        ch_arr, got, feat, dz1, dz2, log_total, out1, out2,
        specs=[SMEM] + [VMEM] * 7,
    )
    back_t, tail_loss = call(back_kernel, [((NAR, T), f32), ((1, T), f32)], got_back, pick)

    is_tail = cluster_id >= 0
    word_local = target - ch * HW
    cluster_local = cluster_id - ch * CW
    local = jnp.where(
        is_tail,
        jnp.where((cluster_local >= 0) & (cluster_local < CW), HW + cluster_local, -1),
        jnp.where((word_local >= 0) & (word_local < HW), word_local, -1),
    )
    gathered, back_t = lax.optimization_barrier((gathered, back_t))
    head = head_call(local.reshape(1, T), hidden, gathered)
    head_parts = lax.all_to_all(head, "ch", split_axis=0, concat_axis=0, tiled=True)
    conv, grad, loss = call(
        conv_kernel,
        [((NCH, NAR, T), bf16), ((NAR, T), f32), ((1, T), f32)],
        head_parts, back_t, tail_loss, pre_gates.transpose(0, 2, 1), gathered[:, HP:],
        scratch=[pltpu.VMEM((CONV, T), bf16)],
        limit=LIMIT,
    )
    conv_parts = lax.all_to_all(conv, "ch", split_axis=0, concat_axis=0, tiled=True)
    (grad_input,) = call(final_kernel, [((T, NAR), bf16)], conv_parts, grad, limit=LIMIT)
    return (loss.reshape(T), grad_input, g_proj1[None], g_proj2[None], g_out1[None], g_out2[None])


def solution(mesh):
    placed = (
        P("tok", None),
        P(None, "tok", "ch"),
        P(None, None, "tok", "ch"),
        P("tok", "ch"),
        P("tok", "ch"),
        P("tok", None, None),
        P("tok", None, None),
        P("tok", None, "ch"),
        P("tok", None, "ch"),
        P("tok"),
        P("tok"),
    )
    return jax.shard_map(
        on_device,
        mesh=mesh,
        in_specs=placed,
        out_specs=(
            P("tok"),
            P("tok", "ch"),
            P("tok", "ch", None),
            P("tok", "ch", None),
            P("tok", None, "ch"),
            P("tok", None, "ch"),
        ),
        check_vma=False,
    )
```

```python
import functools

import jax
import jax.numpy as jnp
from jax import lax
from jax.experimental import pallas as pl
from jax.experimental.pallas import tpu as pltpu
from jax.sharding import PartitionSpec as P

K = 4
LEN = 128
T = 128
D = 1024
OWN = 64
NCH = 8
NAR = 128
HW = 2560
CW = 16
GW = HW + CW
HP = 2688
BLK = 896
CONV = 2 * K * NAR
W1 = 384
W2 = 1152
P1 = 256
P2 = 64
SROW = 16
NEG = -1e30
LIMIT = 24 * 2**20
f32 = jnp.float32
bf16 = jnp.bfloat16
VMEM = pl.BlockSpec(memory_space=pltpu.VMEM)
SMEM = pl.BlockSpec(memory_space=pltpu.SMEM)


def dot(a, b, ca=1, cb=0):
    return lax.dot_general(a, b, (((ca,), (cb,)), ((), ())), preferred_element_type=f32)


def parts3(x):
    hi = x.astype(bf16).astype(f32)
    rest = x - hi
    mid = rest.astype(bf16).astype(f32)
    return [hi, mid, rest - mid]


def iota(shape, axis):
    return lax.broadcasted_iota(jnp.int32, shape, axis)


def call(kernel, outs, *args, specs=None, scratch=(), limit=None, flops=10**7, nbytes=10**6):
    outs = [jax.ShapeDtypeStruct(shape, kind) for shape, kind in outs]
    return pl.pallas_call(
        kernel,
        out_shape=outs,
        in_specs=[VMEM] * len(args) if specs is None else specs,
        out_specs=[VMEM] * len(outs),
        scratch_shapes=list(scratch),
        compiler_params=pltpu.CompilerParams(vmem_limit_bytes=limit),
        cost_estimate=pl.CostEstimate(flops=flops, bytes_accessed=nbytes, transcendentals=0),
    )(*args)


def pack_kernel(head, cluster, conv, out):
    out[:, :HW] = head[...]
    out[:, HW:HP] = jnp.zeros((out.shape[0], HP - HW), bf16)
    out[:, HW:GW] = cluster[...]
    for half in range(2):
        for k in range(K):
            at = HP + (half * K + k) * NAR
            out[:, at : at + NAR] = conv[half, k]


def route_kernel(ch, cid, tgt, hidden, send, pick):
    cid_row = jnp.broadcast_to(cid[...], (T, T))
    cid_col = cid_row.astype(f32).T.astype(jnp.int32)
    word = jnp.broadcast_to(tgt[...], (T, T)).astype(f32).T.astype(jnp.int32)
    owner_row = jnp.where(cid_row >= 0, cid_row // 2, -1)
    owner_col = jnp.where(cid_col >= 0, cid_col // 2, -2)
    before = (owner_col == owner_row) & (iota((T, T), 0) < iota((T, T), 1))
    rank = jnp.sum(before.astype(f32), axis=0, keepdims=True).astype(jnp.int32)
    slot = jnp.where(owner_row >= 0, owner_row * 2 + rank, -1)
    chosen = (iota((T, T), 0) == slot).astype(bf16)
    pick[...] = chosen
    mine = pl.ds(pl.multiple_of(ch[0] * NAR, NAR), NAR)
    send[:, :NAR] = dot(chosen, hidden[:, mine]).astype(bf16)
    lane = iota((T, T), 1)
    tier = jnp.where(cid_col >= 0, cid_col % 2 + 1, 0)
    meta = jnp.where(lane == 0, word // 128, jnp.where(lane == 1, word % 128, jnp.where(lane == 2, tier, 0)))
    send[:, NAR:] = dot(chosen, meta.astype(f32).astype(bf16)).astype(bf16)


def slot_meta(meta):
    meta = meta.astype(f32)
    word = (meta[:, 0:1] * 128.0 + meta[:, 1:2]).astype(jnp.int32)
    tier = meta[:, 2:3].astype(jnp.int32)
    return word, tier


def tail_kernel(ch, got, row_parts, proj1, proj2, out1, out2, feat, part, wide):
    word, tier = slot_meta(got[:, NAR:])
    rows = jnp.concatenate([row_parts[g] for g in range(NCH)], axis=1)
    first = tier == 1
    z1 = dot(rows, proj1[...])
    wide[...] = jnp.zeros_like(wide)
    wide[0, :, :P2] = dot(rows, proj2[...], 1, 1)
    features = jnp.where(first, z1, wide[0]).astype(bf16)
    feat[...] = features

    def local(out, width):
        logits = dot(feat[:, : out.shape[0]], out[...])
        top = jnp.max(logits, axis=1, keepdims=True)
        terms = jnp.exp(logits - top)
        total = jnp.sum(terms, axis=1, keepdims=True)
        hot = iota((T, width), 1) == word - ch[0] * width
        target = jnp.sum(jnp.where(hot, logits, 0.0), axis=1, keepdims=True)
        value = dot(jnp.where(hot, 0.0, terms).astype(bf16), out[...], 1, 1)
        column = dot(hot.astype(f32).astype(bf16), out[...], 1, 1)
        return top, total, target, value, column

    one = local(out1, W1)
    two = list(local(out2, W2))
    for i in (1, 2):
        wide[i, :, :P2] = two[2 + i]
        two[2 + i] = wide[i]
    top, total, target, value, column = [jnp.where(first, a, b) for a, b in zip(one, two)]
    value = value.astype(bf16)
    column = column.astype(bf16)
    lane = iota((T, 128), 1)
    stats = jnp.zeros((T, 128), f32)
    for i, x in enumerate(parts3(top) + parts3(total) + parts3(target)):
        stats = jnp.where(lane == i, x, stats)
    stats = stats.astype(bf16)
    for g in range(NCH):
        part[g, :, :P1] = value
        part[g, :, P1 : 2 * P1] = column
        part[g, :, 2 * P1 :] = stats


def tail_merge_kernel(ch, got, parts, proj1, proj2, dz1, dz2, log_total, back):
    _, tier = slot_meta(got[:, NAR:])
    tops, totals, target = [], [], 0.0
    for g in range(NCH):
        stats = parts[g, :, 2 * P1 :].astype(f32)
        s3 = [stats[:, i : i + 1] for i in range(9)]
        tops.append(s3[0] + s3[1] + s3[2])
        totals.append(s3[3] + s3[4] + s3[5])
        target = target + (s3[6] + s3[7] + s3[8])
    top = functools.reduce(jnp.maximum, tops)
    scales = [jnp.exp(t - top) for t in tops]
    total = sum(s * t for s, t in zip(scales, totals))
    log_all = top + jnp.log(total)
    inverse = 1.0 / total
    value = jnp.zeros((T, P1), f32)
    column = jnp.zeros((T, P1), f32)
    for g in range(NCH):
        value = value + parts[g, :, :P1].astype(f32) * (scales[g] * inverse)
        column = column + parts[g, :, P1 : 2 * P1].astype(f32)
    dz = value + (jnp.exp(target - log_all) - 1.0) * column
    one = jnp.where(tier == 1, dz, 0.0).astype(bf16)
    two = jnp.where(tier == 2, dz, 0.0).astype(bf16)
    dz1[...] = one
    dz2[...] = two
    log_total[...] = jnp.broadcast_to(log_all, (T, 128))
    mine = pl.ds(pl.multiple_of(ch[0] * NAR, NAR), NAR)
    back[:, :NAR] = (dot(one, proj1[mine, :], 1, 1) + dot(two[:, :P2], proj2[:, mine])).astype(bf16)
    loss = jnp.where(tier > 0, log_all - target, 0.0)
    lane = iota((T, 128), 1)
    tail = jnp.zeros((T, 128), f32)
    for i, x in enumerate(parts3(loss)):
        tail = jnp.where(lane == i, x, tail)
    back[:, NAR:] = tail.astype(bf16)


def tail_grad_kernel(ch, got, feat, dz1, dz2, log_total, out1, out2, g_out1, g_out2, g_proj1, g_proj2):
    word, tier = slot_meta(got[:, NAR:])
    rows_part = got[:, :NAR]
    features = feat[...]
    log_all = log_total[:, 0:1]

    def slope(out, width, which):
        logits = dot(feat[:, : out.shape[0]], out[...])
        hot = (iota((T, width), 1) == word - ch[0] * width).astype(f32)
        return jnp.where(tier == which, jnp.exp(logits - log_all) - hot, 0.0).astype(bf16)

    g_out1[...] = dot(features, slope(out1, W1, 1), 0, 0)
    g_out2[...] = dot(feat[:, :P2], slope(out2, W2, 2), 0, 0)
    g_proj1[...] = dot(rows_part, dz1[...], 0, 0)
    g_proj2[...] = dot(dz2[:, :P2], rows_part, 0, 0)


def back_kernel(got, pick, back_t, loss):
    back_t[...] = dot(got[:, :NAR], pick[...], 0, 0)
    terms = dot(got[:, NAR:], pick[...], 0, 0)
    loss[...] = terms[0:1] + terms[1:2] + terms[2:3]


def head_kernel(col, hidden, weight, out, acc, stat):
    step = pl.program_id(0)

    @pl.when(step == 0)
    def _():
        acc[...] = jnp.zeros_like(acc)
        stat[0:1, :] = jnp.full((1, T), NEG, f32)
        stat[1:2, :] = jnp.zeros((1, T), f32)
        stat[2:3, :] = jnp.zeros((1, T), f32)

    logits = dot(hidden[...], weight[...]).T
    index = iota((BLK, T), 0) + step * BLK
    logits = jnp.where(index < GW, logits, NEG)
    old = stat[0:1, :]
    top = jnp.maximum(old, jnp.max(logits, axis=0, keepdims=True))
    scale = jnp.exp(old - top)
    terms = jnp.exp(logits - top)
    hot = index == col[...]
    stat[0:1, :] = top
    stat[1:2, :] = stat[1:2, :] * scale + jnp.sum(terms, axis=0, keepdims=True)
    stat[2:3, :] = stat[2:3, :] + jnp.sum(jnp.where(hot, logits, 0.0), axis=0, keepdims=True)
    right = jnp.concatenate([jnp.where(hot, 0.0, terms), hot.astype(f32)], axis=1).astype(bf16)
    new = dot(weight[...], right)
    acc[:, :T] = acc[:, :T] * scale + new[:, :T]
    acc[:, T:] = acc[:, T:] + new[:, T:]

    @pl.when(step == pl.num_programs(0) - 1)
    def _():
        line = iota((SROW, 2 * T), 0)
        stats = jnp.zeros((SROW, 2 * T), f32)
        rows = parts3(stat[0:1, :]) + parts3(stat[1:2, :]) + parts3(stat[2:3, :])
        for i, x in enumerate(rows):
            stats = jnp.where(line == i, jnp.concatenate([x, x], axis=1), stats)
        for g in range(NCH):
            out[g, :NAR, :] = acc[g * NAR : (g + 1) * NAR, :].astype(bf16)
            out[g, NAR:, :] = stats.astype(bf16)


def head_call(col, hidden, weight):
    return pl.pallas_call(
        head_kernel,
        out_shape=jax.ShapeDtypeStruct((NCH, NAR + SROW, 2 * T), bf16),
        grid=(HP // BLK,),
        in_specs=[
            pl.BlockSpec((1, T), lambda i: (0, 0)),
            pl.BlockSpec((T, D), lambda i: (0, 0)),
            pl.BlockSpec((D, BLK), lambda i: (0, i)),
        ],
        out_specs=pl.BlockSpec((NCH, NAR + SROW, 2 * T), lambda i: (0, 0, 0)),
        scratch_shapes=[pltpu.VMEM((D, 2 * T), f32), pltpu.VMEM((8, T), f32)],
        compiler_params=pltpu.CompilerParams(dimension_semantics=("arbitrary",)),
        cost_estimate=pl.CostEstimate(flops=2 * 10**9, bytes_accessed=6 * 10**6, transcendentals=0),
    )(col, hidden, weight)


def conv_kernel(parts, back_t, tail_loss, gates, weight, conv, grad, loss, taps):
    tops, totals, target = [], [], 0.0
    for g in range(NCH):
        stats = parts[g, NAR:, :T].astype(f32)
        s3 = [stats[i : i + 1] for i in range(9)]
        tops.append(s3[0] + s3[1] + s3[2])
        totals.append(s3[3] + s3[4] + s3[5])
        target = target + (s3[6] + s3[7] + s3[8])
    top = functools.reduce(jnp.maximum, tops)
    scales = [jnp.exp(t - top) for t in tops]
    total = sum(s * t for s, t in zip(scales, totals))
    log_all = top + jnp.log(total)
    inverse = 1.0 / total
    loss[...] = log_all - target + tail_loss[...]
    dh = back_t[...]
    column = jnp.zeros((NAR, T), f32)
    for g in range(NCH):
        dh = dh + parts[g, :NAR, :T].astype(f32) * (scales[g] * inverse)
        column = column + parts[g, :NAR, T:].astype(f32)
    dh = dh + (jnp.exp(target - log_all) - 1.0) * column
    grad[...] = dh
    a = gates[0].astype(f32)
    sig = 1.0 / (1.0 + jnp.exp(-gates[1].astype(f32)))
    da = dh * sig
    db = da * a * (1.0 - sig)
    lane = iota((NAR, T), 1)
    for half, value in enumerate((da, db)):
        for k in range(K):
            moved = value if k == 0 else jnp.where(lane < T - k, pltpu.roll(value, T - k, 1), 0.0)
            at = (half * K + k) * NAR
            taps[at : at + NAR, :] = moved.astype(bf16)
    total_conv = dot(weight[...], taps[...])
    for g in range(NCH):
        conv[g] = total_conv[g * NAR : (g + 1) * NAR].astype(bf16)


def final_kernel(parts, grad, out):
    total = grad[...]
    for g in range(NCH):
        total = total + parts[g].astype(f32)
    out[...] = total.T.astype(bf16)


def on_device(hidden, pre_gates, conv_weight, head_weight, cluster_weight, tail1_proj, tail2_proj, tail1_out, tail2_out, cluster_id, target):
    ch = lax.axis_index("ch").astype(jnp.int32)
    ch_arr = ch.reshape(1)
    (packed,) = call(pack_kernel, [((head_weight.shape[0], HP + CONV), bf16)], head_weight, cluster_weight, conv_weight)
    gathered = lax.all_gather(packed, "tok", axis=0, tiled=True)

    send, pick = call(
        route_kernel,
        [((T, NAR + 128), bf16), ((T, T), bf16)],
        ch_arr,
        cluster_id.reshape(1, T),
        target.reshape(1, T),
        hidden,
        specs=[SMEM] + [VMEM] * 3,
    )
    got = lax.all_to_all(send.reshape(OWN, 2, NAR + 128), "tok", split_axis=0, concat_axis=0, tiled=True).reshape(T, NAR + 128)
    row_parts = lax.all_gather(got[:, :NAR], "ch")
    proj1 = tail1_proj[0]
    proj2 = tail2_proj[0].T
    out1 = tail1_out[0]
    out2 = tail2_out[0]
    feat, part = call(
        tail_kernel,
        [((T, P1), bf16), ((NCH, T, 2 * P1 + 128), bf16)],
        ch_arr, got, row_parts, proj1, proj2, out1, out2,
        specs=[SMEM] + [VMEM] * 6,
        scratch=[pltpu.VMEM((3, T, P1), f32)],
    )
    parts = lax.all_to_all(part, "ch", split_axis=0, concat_axis=0, tiled=True)
    dz1, dz2, log_total, back = call(
        tail_merge_kernel,
        [((T, P1), bf16), ((T, P1), bf16), ((T, 128), f32), ((T, NAR + 128), bf16)],
        ch_arr, got, parts, proj1, proj2,
        specs=[SMEM] + [VMEM] * 4,
    )
    got_back = lax.all_to_all(back.reshape(OWN, 2, NAR + 128), "tok", split_axis=0, concat_axis=0, tiled=True).reshape(T, NAR + 128)
    g_out1, g_out2, g_proj1, g_proj2 = call(
        tail_grad_kernel,
        [((P1, W1), f32), ((P2, W2), f32), ((NAR, P1), f32), ((P2, NAR), f32)],
        ch_arr, got, feat, dz1, dz2, log_total, out1, out2,
        specs=[SMEM] + [VMEM] * 7,
    )
    back_t, tail_loss = call(back_kernel, [((NAR, T), f32), ((1, T), f32)], got_back, pick)

    is_tail = cluster_id >= 0
    word_local = target - ch * HW
    cluster_local = cluster_id - ch * CW
    local = jnp.where(
        is_tail,
        jnp.where((cluster_local >= 0) & (cluster_local < CW), HW + cluster_local, -1),
        jnp.where((word_local >= 0) & (word_local < HW), word_local, -1),
    )
    gathered, back_t = lax.optimization_barrier((gathered, back_t))
    head = head_call(local.reshape(1, T), hidden, gathered)
    head_parts = lax.all_to_all(head, "ch", split_axis=0, concat_axis=0, tiled=True)
    conv, grad, loss = call(
        conv_kernel,
        [((NCH, NAR, T), bf16), ((NAR, T), f32), ((1, T), f32)],
        head_parts, back_t, tail_loss, pre_gates.transpose(0, 2, 1), gathered[:, HP:],
        scratch=[pltpu.VMEM((CONV, T), bf16)],
        limit=LIMIT,
    )
    conv_parts = lax.all_to_all(conv, "ch", split_axis=0, concat_axis=0, tiled=True)
    (grad_input,) = call(final_kernel, [((T, NAR), bf16)], conv_parts, grad, limit=LIMIT)
    return (loss.reshape(T), grad_input, g_proj1[None], g_proj2.T[None], g_out1[None], g_out2[None])


def solution(mesh):
    placed = (
        P("tok", None),
        P(None, "tok", "ch"),
        P(None, None, "tok", "ch"),
        P("tok", "ch"),
        P("tok", "ch"),
        P("tok", None, None),
        P("tok", None, None),
        P("tok", None, "ch"),
        P("tok", None, "ch"),
        P("tok"),
        P("tok"),
    )
    return jax.shard_map(
        on_device,
        mesh=mesh,
        in_specs=placed,
        out_specs=(
            P("tok"),
            P("tok", "ch"),
            P("tok", "ch", None),
            P("tok", "ch", None),
            P("tok", None, "ch"),
            P("tok", None, "ch"),
        ),
        check_vma=False,
    )
```

```python
import functools

import jax
import jax.numpy as jnp
from jax import lax
from jax.experimental import pallas as pl
from jax.experimental.pallas import tpu as pltpu
from jax.sharding import PartitionSpec as P

K = 4
LEN = 128
T = 128
D = 1024
OWN = 64
NCH = 8
NAR = 128
HW = 2560
CW = 16
GW = HW + CW
HP = 2688
BLK = 896
CONV = 2 * K * NAR
W1 = 384
W2 = 1152
P1 = 256
P2 = 64
SROW = 8
NEG = -1e30
LIMIT = 24 * 2**20
f32 = jnp.float32
bf16 = jnp.bfloat16
VMEM = pl.BlockSpec(memory_space=pltpu.VMEM)
SMEM = pl.BlockSpec(memory_space=pltpu.SMEM)


def dot(a, b, ca=1, cb=0):
    return lax.dot_general(a, b, (((ca,), (cb,)), ((), ())), preferred_element_type=f32)


def parts3(x):
    hi = x.astype(bf16).astype(f32)
    rest = x - hi
    mid = rest.astype(bf16).astype(f32)
    return [hi, mid, rest - mid]


def iota(shape, axis):
    return lax.broadcasted_iota(jnp.int32, shape, axis)


def call(kernel, outs, *args, specs=None, scratch=(), limit=None, flops=10**7, nbytes=10**6):
    outs = [jax.ShapeDtypeStruct(shape, kind) for shape, kind in outs]
    return pl.pallas_call(
        kernel,
        out_shape=outs,
        in_specs=[VMEM] * len(args) if specs is None else specs,
        out_specs=[VMEM] * len(outs),
        scratch_shapes=list(scratch),
        compiler_params=pltpu.CompilerParams(vmem_limit_bytes=limit),
        cost_estimate=pl.CostEstimate(flops=flops, bytes_accessed=nbytes, transcendentals=0),
    )(*args)


def pack_kernel(head, cluster, conv, out):
    out[:, :HW] = head[...]
    out[:, HW:HP] = jnp.zeros((out.shape[0], HP - HW), bf16)
    out[:, HW:GW] = cluster[...]
    for half in range(2):
        for k in range(K):
            at = HP + (half * K + k) * NAR
            out[:, at : at + NAR] = conv[half, k]


def route_kernel(ch, cid, tgt, hidden, send, pick):
    cid_row = jnp.broadcast_to(cid[...], (T, T))
    cid_col = cid_row.astype(f32).T.astype(jnp.int32)
    word = jnp.broadcast_to(tgt[...], (T, T)).astype(f32).T.astype(jnp.int32)
    owner_row = jnp.where(cid_row >= 0, cid_row // 2, -1)
    owner_col = jnp.where(cid_col >= 0, cid_col // 2, -2)
    before = (owner_col == owner_row) & (iota((T, T), 0) < iota((T, T), 1))
    rank = jnp.sum(before.astype(f32), axis=0, keepdims=True).astype(jnp.int32)
    slot = jnp.where(owner_row >= 0, owner_row * 2 + rank, -1)
    chosen = (iota((T, T), 0) == slot).astype(bf16)
    pick[...] = chosen
    mine = pl.ds(pl.multiple_of(ch[0] * NAR, NAR), NAR)
    send[:, :NAR] = dot(chosen, hidden[:, mine]).astype(bf16)
    lane = iota((T, T), 1)
    tier = jnp.where(cid_col >= 0, cid_col % 2 + 1, 0)
    meta = jnp.where(lane == 0, word // 128, jnp.where(lane == 1, word % 128, jnp.where(lane == 2, tier, 0)))
    send[:, NAR:] = dot(chosen, meta.astype(f32).astype(bf16)).astype(bf16)


def slot_meta(meta):
    meta = meta.astype(f32)
    word = (meta[:, 0:1] * 128.0 + meta[:, 1:2]).astype(jnp.int32)
    tier = meta[:, 2:3].astype(jnp.int32)
    return word, tier


def tail_kernel(ch, got, row_parts, proj1, proj2, out1, out2, feat, part, wide):
    word, tier = slot_meta(got[:, NAR:])
    rows = jnp.concatenate([row_parts[g] for g in range(NCH)], axis=1)
    first = tier == 1
    z1 = dot(rows, proj1[...])
    wide[...] = jnp.zeros_like(wide)
    wide[0, :, :P2] = dot(rows, proj2[...], 1, 1)
    features = jnp.where(first, z1, wide[0]).astype(bf16)
    feat[...] = features

    def local(out, width):
        logits = dot(feat[:, : out.shape[0]], out[...])
        top = jnp.max(logits, axis=1, keepdims=True)
        terms = jnp.exp(logits - top)
        total = jnp.sum(terms, axis=1, keepdims=True)
        hot = iota((T, width), 1) == word - ch[0] * width
        target = jnp.sum(jnp.where(hot, logits, 0.0), axis=1, keepdims=True)
        value = dot(jnp.where(hot, 0.0, terms).astype(bf16), out[...], 1, 1)
        column = dot(hot.astype(f32).astype(bf16), out[...], 1, 1)
        return top, total, target, value, column

    one = local(out1, W1)
    two = list(local(out2, W2))
    for i in (1, 2):
        wide[i, :, :P2] = two[2 + i]
        two[2 + i] = wide[i]
    top, total, target, value, column = [jnp.where(first, a, b) for a, b in zip(one, two)]
    value = value.astype(bf16)
    column = column.astype(bf16)
    lane = iota((T, 128), 1)
    stats = jnp.zeros((T, 128), f32)
    for i, x in enumerate(parts3(top) + parts3(total) + parts3(target)):
        stats = jnp.where(lane == i, x, stats)
    stats = stats.astype(bf16)
    for g in range(NCH):
        part[g, :, :P1] = value
        part[g, :, P1 : 2 * P1] = column
        part[g, :, 2 * P1 :] = stats


def tail_merge_kernel(ch, got, parts, proj1, proj2, dz1, dz2, log_total, back):
    _, tier = slot_meta(got[:, NAR:])
    tops, totals, target = [], [], 0.0
    for g in range(NCH):
        stats = parts[g, :, 2 * P1 :].astype(f32)
        s3 = [stats[:, i : i + 1] for i in range(9)]
        tops.append(s3[0] + s3[1] + s3[2])
        totals.append(s3[3] + s3[4] + s3[5])
        target = target + (s3[6] + s3[7] + s3[8])
    top = functools.reduce(jnp.maximum, tops)
    scales = [jnp.exp(t - top) for t in tops]
    total = sum(s * t for s, t in zip(scales, totals))
    log_all = top + jnp.log(total)
    inverse = 1.0 / total
    value = jnp.zeros((T, P1), f32)
    column = jnp.zeros((T, P1), f32)
    for g in range(NCH):
        value = value + parts[g, :, :P1].astype(f32) * (scales[g] * inverse)
        column = column + parts[g, :, P1 : 2 * P1].astype(f32)
    dz = value + (jnp.exp(target - log_all) - 1.0) * column
    one = jnp.where(tier == 1, dz, 0.0).astype(bf16)
    two = jnp.where(tier == 2, dz, 0.0).astype(bf16)
    dz1[...] = one
    dz2[...] = two
    log_total[...] = jnp.broadcast_to(log_all, (T, 128))
    mine = pl.ds(pl.multiple_of(ch[0] * NAR, NAR), NAR)
    back[:, :NAR] = (dot(one, proj1[mine, :], 1, 1) + dot(two[:, :P2], proj2[:, mine])).astype(bf16)
    loss = jnp.where(tier > 0, log_all - target, 0.0)
    lane = iota((T, 128), 1)
    tail = jnp.zeros((T, 128), f32)
    for i, x in enumerate(parts3(loss)):
        tail = jnp.where(lane == i, x, tail)
    back[:, NAR:] = tail.astype(bf16)


def tail_grad_kernel(ch, got, feat, dz1, dz2, log_total, out1, out2, g_out1, g_out2, g_proj1, g_proj2):
    word, tier = slot_meta(got[:, NAR:])
    rows_part = got[:, :NAR]
    features = feat[...]
    log_all = log_total[:, 0:1]

    def slope(out, width, which):
        logits = dot(feat[:, : out.shape[0]], out[...])
        hot = (iota((T, width), 1) == word - ch[0] * width).astype(f32)
        return jnp.where(tier == which, jnp.exp(logits - log_all) - hot, 0.0).astype(bf16)

    g_out1[...] = dot(features, slope(out1, W1, 1), 0, 0)
    g_out2[...] = dot(feat[:, :P2], slope(out2, W2, 2), 0, 0)
    g_proj1[...] = dot(rows_part, dz1[...], 0, 0)
    g_proj2[...] = dot(dz2[:, :P2], rows_part, 0, 0)


def back_kernel(got, pick, back_t, loss):
    back_t[...] = dot(got[:, :NAR], pick[...], 0, 0)
    terms = dot(got[:, NAR:], pick[...], 0, 0)
    loss[...] = terms[0:1] + terms[1:2] + terms[2:3]


def head_kernel(col, hidden, weight, out, acc, stat):
    step = pl.program_id(0)

    @pl.when(step == 0)
    def _():
        acc[...] = jnp.zeros_like(acc)
        stat[0:1, :] = jnp.full((1, T), NEG, f32)
        stat[1:2, :] = jnp.zeros((1, T), f32)
        stat[2:3, :] = jnp.zeros((1, T), f32)

    logits = dot(hidden[...], weight[...]).T
    index = iota((BLK, T), 0) + step * BLK
    logits = jnp.where(index < GW, logits, NEG)
    old = stat[0:1, :]
    top = jnp.maximum(old, jnp.max(logits, axis=0, keepdims=True))
    scale = jnp.exp(old - top)
    terms = jnp.exp(logits - top)
    hot = index == col[...]
    stat[0:1, :] = top
    stat[1:2, :] = stat[1:2, :] * scale + jnp.sum(terms, axis=0, keepdims=True)
    stat[2:3, :] = stat[2:3, :] + jnp.sum(jnp.where(hot, logits, 0.0), axis=0, keepdims=True)
    right = jnp.concatenate([jnp.where(hot, 0.0, terms), hot.astype(f32)], axis=1).astype(bf16)
    new = dot(weight[...], right)
    acc[:, :T] = acc[:, :T] * scale + new[:, :T]
    acc[:, T:] = acc[:, T:] + new[:, T:]

    @pl.when(step == pl.num_programs(0) - 1)
    def _():
        line = iota((SROW, 2 * T), 0)
        stats = jnp.zeros((SROW, 2 * T), f32)
        rows = parts3(stat[0:1, :]) + parts3(stat[1:2, :]) + parts3(stat[2:3, :])
        rows.append(jnp.zeros((1, T), f32))
        for i in range(len(rows) // 2):
            stats = jnp.where(line == i, jnp.concatenate(rows[2 * i : 2 * i + 2], axis=1), stats)
        for g in range(NCH):
            out[g, :NAR, :] = acc[g * NAR : (g + 1) * NAR, :].astype(bf16)
            out[g, NAR:, :] = stats.astype(bf16)


def head_call(col, hidden, weight):
    return pl.pallas_call(
        head_kernel,
        out_shape=jax.ShapeDtypeStruct((NCH, NAR + SROW, 2 * T), bf16),
        grid=(HP // BLK,),
        in_specs=[
            pl.BlockSpec((1, T), lambda i: (0, 0)),
            pl.BlockSpec((T, D), lambda i: (0, 0)),
            pl.BlockSpec((D, BLK), lambda i: (0, i)),
        ],
        out_specs=pl.BlockSpec((NCH, NAR + SROW, 2 * T), lambda i: (0, 0, 0)),
        scratch_shapes=[pltpu.VMEM((D, 2 * T), f32), pltpu.VMEM((8, T), f32)],
        compiler_params=pltpu.CompilerParams(dimension_semantics=("arbitrary",)),
        cost_estimate=pl.CostEstimate(flops=2 * 10**9, bytes_accessed=6 * 10**6, transcendentals=0),
    )(col, hidden, weight)


def conv_kernel(parts, back_t, tail_loss, gates, weight, conv, grad, loss, taps):
    tops, totals, target = [], [], 0.0
    for g in range(NCH):
        stats = parts[g, NAR:, :].astype(f32)
        s3 = [stats[i // 2 : i // 2 + 1, i % 2 * T : (i % 2 + 1) * T] for i in range(9)]
        tops.append(s3[0] + s3[1] + s3[2])
        totals.append(s3[3] + s3[4] + s3[5])
        target = target + (s3[6] + s3[7] + s3[8])
    top = functools.reduce(jnp.maximum, tops)
    scales = [jnp.exp(t - top) for t in tops]
    total = sum(s * t for s, t in zip(scales, totals))
    log_all = top + jnp.log(total)
    inverse = 1.0 / total
    loss[...] = log_all - target + tail_loss[...]
    dh = back_t[...]
    column = jnp.zeros((NAR, T), f32)
    for g in range(NCH):
        dh = dh + parts[g, :NAR, :T].astype(f32) * (scales[g] * inverse)
        column = column + parts[g, :NAR, T:].astype(f32)
    dh = dh + (jnp.exp(target - log_all) - 1.0) * column
    grad[...] = dh
    a = gates[0].astype(f32)
    sig = 1.0 / (1.0 + jnp.exp(-gates[1].astype(f32)))
    da = dh * sig
    db = da * a * (1.0 - sig)
    lane = iota((NAR, T), 1)
    for half, value in enumerate((da, db)):
        for k in range(K):
            moved = value if k == 0 else jnp.where(lane < T - k, pltpu.roll(value, T - k, 1), 0.0)
            at = (half * K + k) * NAR
            taps[at : at + NAR, :] = moved.astype(bf16)
    total_conv = dot(weight[...], taps[...])
    for g in range(NCH):
        conv[g] = total_conv[g * NAR : (g + 1) * NAR].astype(bf16)


def final_kernel(parts, grad, out):
    total = grad[...]
    for g in range(NCH):
        total = total + parts[g].astype(f32)
    out[...] = total.T.astype(bf16)


def on_device(hidden, pre_gates, conv_weight, head_weight, cluster_weight, tail1_proj, tail2_proj, tail1_out, tail2_out, cluster_id, target):
    ch = lax.axis_index("ch").astype(jnp.int32)
    ch_arr = ch.reshape(1)
    (packed,) = call(pack_kernel, [((head_weight.shape[0], HP + CONV), bf16)], head_weight, cluster_weight, conv_weight)
    gathered = lax.all_gather(packed, "tok", axis=0, tiled=True)

    send, pick = call(
        route_kernel,
        [((T, NAR + 128), bf16), ((T, T), bf16)],
        ch_arr,
        cluster_id.reshape(1, T),
        target.reshape(1, T),
        hidden,
        specs=[SMEM] + [VMEM] * 3,
    )
    got = lax.all_to_all(send.reshape(OWN, 2, NAR + 128), "tok", split_axis=0, concat_axis=0, tiled=True).reshape(T, NAR + 128)
    row_parts = lax.all_gather(got[:, :NAR], "ch")
    proj1 = tail1_proj[0]
    proj2 = tail2_proj[0].T
    out1 = tail1_out[0]
    out2 = tail2_out[0]
    feat, part = call(
        tail_kernel,
        [((T, P1), bf16), ((NCH, T, 2 * P1 + 128), bf16)],
        ch_arr, got, row_parts, proj1, proj2, out1, out2,
        specs=[SMEM] + [VMEM] * 6,
        scratch=[pltpu.VMEM((3, T, P1), f32)],
    )
    parts = lax.all_to_all(part, "ch", split_axis=0, concat_axis=0, tiled=True)
    dz1, dz2, log_total, back = call(
        tail_merge_kernel,
        [((T, P1), bf16), ((T, P1), bf16), ((T, 128), f32), ((T, NAR + 128), bf16)],
        ch_arr, got, parts, proj1, proj2,
        specs=[SMEM] + [VMEM] * 4,
    )
    got_back = lax.all_to_all(back.reshape(OWN, 2, NAR + 128), "tok", split_axis=0, concat_axis=0, tiled=True).reshape(T, NAR + 128)
    g_out1, g_out2, g_proj1, g_proj2 = call(
        tail_grad_kernel,
        [((P1, W1), f32), ((P2, W2), f32), ((NAR, P1), f32), ((P2, NAR), f32)],
        ch_arr, got, feat, dz1, dz2, log_total, out1, out2,
        specs=[SMEM] + [VMEM] * 7,
    )
    back_t, tail_loss = call(back_kernel, [((NAR, T), f32), ((1, T), f32)], got_back, pick)

    is_tail = cluster_id >= 0
    word_local = target - ch * HW
    cluster_local = cluster_id - ch * CW
    local = jnp.where(
        is_tail,
        jnp.where((cluster_local >= 0) & (cluster_local < CW), HW + cluster_local, -1),
        jnp.where((word_local >= 0) & (word_local < HW), word_local, -1),
    )
    gathered, back_t = lax.optimization_barrier((gathered, back_t))
    head = head_call(local.reshape(1, T), hidden, gathered)
    head_parts = lax.all_to_all(head, "ch", split_axis=0, concat_axis=0, tiled=True)
    conv, grad, loss = call(
        conv_kernel,
        [((NCH, NAR, T), bf16), ((NAR, T), f32), ((1, T), f32)],
        head_parts, back_t, tail_loss, pre_gates.transpose(0, 2, 1), gathered[:, HP:],
        scratch=[pltpu.VMEM((CONV, T), bf16)],
        limit=LIMIT,
    )
    conv_parts = lax.all_to_all(conv, "ch", split_axis=0, concat_axis=0, tiled=True)
    (grad_input,) = call(final_kernel, [((T, NAR), bf16)], conv_parts, grad, limit=LIMIT)
    return (loss.reshape(T), grad_input, g_proj1[None], g_proj2.T[None], g_out1[None], g_out2[None])


def solution(mesh):
    placed = (
        P("tok", None),
        P(None, "tok", "ch"),
        P(None, None, "tok", "ch"),
        P("tok", "ch"),
        P("tok", "ch"),
        P("tok", None, None),
        P("tok", None, None),
        P("tok", None, "ch"),
        P("tok", None, "ch"),
        P("tok"),
        P("tok"),
    )
    return jax.shard_map(
        on_device,
        mesh=mesh,
        in_specs=placed,
        out_specs=(
            P("tok"),
            P("tok", "ch"),
            P("tok", "ch", None),
            P("tok", "ch", None),
            P("tok", None, "ch"),
            P("tok", None, "ch"),
        ),
        check_vma=False,
    )
```

```python
import functools

import jax
import jax.numpy as jnp
from jax import lax
from jax.experimental import pallas as pl
from jax.experimental.pallas import tpu as pltpu
from jax.sharding import PartitionSpec as P

K = 4
LEN = 128
T = 128
D = 1024
OWN = 64
NCH = 8
NAR = 128
HW = 2560
CW = 16
GW = HW + CW
HP = 2688
BLK = 1280
TAIL = 128
CONV = 2 * K * NAR
W1 = 384
W2 = 1152
P1 = 256
P2 = 64
SROW = 8
NEG = -1e30
LIMIT = 24 * 2**20
f32 = jnp.float32
bf16 = jnp.bfloat16
VMEM = pl.BlockSpec(memory_space=pltpu.VMEM)
SMEM = pl.BlockSpec(memory_space=pltpu.SMEM)


def dot(a, b, ca=1, cb=0):
    return lax.dot_general(a, b, (((ca,), (cb,)), ((), ())), preferred_element_type=f32)


def parts3(x):
    hi = x.astype(bf16).astype(f32)
    rest = x - hi
    mid = rest.astype(bf16).astype(f32)
    return [hi, mid, rest - mid]


def iota(shape, axis):
    return lax.broadcasted_iota(jnp.int32, shape, axis)


def call(kernel, outs, *args, specs=None, scratch=(), limit=None, flops=10**7, nbytes=10**6):
    outs = [jax.ShapeDtypeStruct(shape, kind) for shape, kind in outs]
    return pl.pallas_call(
        kernel,
        out_shape=outs,
        in_specs=[VMEM] * len(args) if specs is None else specs,
        out_specs=[VMEM] * len(outs),
        scratch_shapes=list(scratch),
        compiler_params=pltpu.CompilerParams(vmem_limit_bytes=limit),
        cost_estimate=pl.CostEstimate(flops=flops, bytes_accessed=nbytes, transcendentals=0),
    )(*args)


def pack_kernel(head, cluster, conv, out):
    out[:, :HW] = head[...]
    out[:, HW:HP] = jnp.zeros((out.shape[0], HP - HW), bf16)
    out[:, HW:GW] = cluster[...]
    for half in range(2):
        for k in range(K):
            at = HP + (half * K + k) * NAR
            out[:, at : at + NAR] = conv[half, k]


def route_kernel(ch, cid, tgt, hidden, send, pick):
    cid_row = jnp.broadcast_to(cid[...], (T, T))
    cid_col = cid_row.astype(f32).T.astype(jnp.int32)
    word = jnp.broadcast_to(tgt[...], (T, T)).astype(f32).T.astype(jnp.int32)
    owner_row = jnp.where(cid_row >= 0, cid_row // 2, -1)
    owner_col = jnp.where(cid_col >= 0, cid_col // 2, -2)
    before = (owner_col == owner_row) & (iota((T, T), 0) < iota((T, T), 1))
    rank = jnp.sum(before.astype(f32), axis=0, keepdims=True).astype(jnp.int32)
    slot = jnp.where(owner_row >= 0, owner_row * 2 + rank, -1)
    chosen = (iota((T, T), 0) == slot).astype(bf16)
    pick[...] = chosen
    mine = pl.ds(pl.multiple_of(ch[0] * NAR, NAR), NAR)
    send[:, :NAR] = dot(chosen, hidden[:, mine]).astype(bf16)
    lane = iota((T, T), 1)
    tier = jnp.where(cid_col >= 0, cid_col % 2 + 1, 0)
    meta = jnp.where(lane == 0, word // 128, jnp.where(lane == 1, word % 128, jnp.where(lane == 2, tier, 0)))
    send[:, NAR:] = dot(chosen, meta.astype(f32).astype(bf16)).astype(bf16)


def slot_meta(meta):
    meta = meta.astype(f32)
    word = (meta[:, 0:1] * 128.0 + meta[:, 1:2]).astype(jnp.int32)
    tier = meta[:, 2:3].astype(jnp.int32)
    return word, tier


def tail_kernel(ch, got, row_parts, proj1, proj2, out1, out2, feat, part, wide):
    word, tier = slot_meta(got[:, NAR:])
    rows = jnp.concatenate([row_parts[g] for g in range(NCH)], axis=1)
    first = tier == 1
    z1 = dot(rows, proj1[...])
    wide[...] = jnp.zeros_like(wide)
    wide[0, :, :P2] = dot(rows, proj2[...], 1, 1)
    features = jnp.where(first, z1, wide[0]).astype(bf16)
    feat[...] = features

    def local(out, width):
        logits = dot(feat[:, : out.shape[0]], out[...])
        top = jnp.max(logits, axis=1, keepdims=True)
        terms = jnp.exp(logits - top)
        total = jnp.sum(terms, axis=1, keepdims=True)
        hot = iota((T, width), 1) == word - ch[0] * width
        target = jnp.sum(jnp.where(hot, logits, 0.0), axis=1, keepdims=True)
        value = dot(jnp.where(hot, 0.0, terms).astype(bf16), out[...], 1, 1)
        column = dot(hot.astype(f32).astype(bf16), out[...], 1, 1)
        return top, total, target, value, column

    one = local(out1, W1)
    two = list(local(out2, W2))
    for i in (1, 2):
        wide[i, :, :P2] = two[2 + i]
        two[2 + i] = wide[i]
    top, total, target, value, column = [jnp.where(first, a, b) for a, b in zip(one, two)]
    value = value.astype(bf16)
    column = column.astype(bf16)
    lane = iota((T, 128), 1)
    stats = jnp.zeros((T, 128), f32)
    for i, x in enumerate(parts3(top) + parts3(total) + parts3(target)):
        stats = jnp.where(lane == i, x, stats)
    stats = stats.astype(bf16)
    for g in range(NCH):
        part[g, :, :P1] = value
        part[g, :, P1 : 2 * P1] = column
        part[g, :, 2 * P1 :] = stats


def tail_merge_kernel(ch, got, parts, proj1, proj2, dz1, dz2, log_total, back):
    _, tier = slot_meta(got[:, NAR:])
    tops, totals, target = [], [], 0.0
    for g in range(NCH):
        stats = parts[g, :, 2 * P1 :].astype(f32)
        s3 = [stats[:, i : i + 1] for i in range(9)]
        tops.append(s3[0] + s3[1] + s3[2])
        totals.append(s3[3] + s3[4] + s3[5])
        target = target + (s3[6] + s3[7] + s3[8])
    top = functools.reduce(jnp.maximum, tops)
    scales = [jnp.exp(t - top) for t in tops]
    total = sum(s * t for s, t in zip(scales, totals))
    log_all = top + jnp.log(total)
    inverse = 1.0 / total
    value = jnp.zeros((T, P1), f32)
    column = jnp.zeros((T, P1), f32)
    for g in range(NCH):
        value = value + parts[g, :, :P1].astype(f32) * (scales[g] * inverse)
        column = column + parts[g, :, P1 : 2 * P1].astype(f32)
    dz = value + (jnp.exp(target - log_all) - 1.0) * column
    one = jnp.where(tier == 1, dz, 0.0).astype(bf16)
    two = jnp.where(tier == 2, dz, 0.0).astype(bf16)
    dz1[...] = one
    dz2[...] = two
    log_total[...] = jnp.broadcast_to(log_all, (T, 128))
    mine = pl.ds(pl.multiple_of(ch[0] * NAR, NAR), NAR)
    back[:, :NAR] = (dot(one, proj1[mine, :], 1, 1) + dot(two[:, :P2], proj2[:, mine])).astype(bf16)
    loss = jnp.where(tier > 0, log_all - target, 0.0)
    lane = iota((T, 128), 1)
    tail = jnp.zeros((T, 128), f32)
    for i, x in enumerate(parts3(loss)):
        tail = jnp.where(lane == i, x, tail)
    back[:, NAR:] = tail.astype(bf16)


def tail_grad_kernel(ch, got, feat, dz1, dz2, log_total, out1, out2, g_out1, g_out2, g_proj1, g_proj2):
    word, tier = slot_meta(got[:, NAR:])
    rows_part = got[:, :NAR]
    features = feat[...]
    log_all = log_total[:, 0:1]

    def slope(out, width, which):
        logits = dot(feat[:, : out.shape[0]], out[...])
        hot = (iota((T, width), 1) == word - ch[0] * width).astype(f32)
        return jnp.where(tier == which, jnp.exp(logits - log_all) - hot, 0.0).astype(bf16)

    g_out1[...] = dot(features, slope(out1, W1, 1), 0, 0)
    g_out2[...] = dot(feat[:, :P2], slope(out2, W2, 2), 0, 0)
    g_proj1[...] = dot(rows_part, dz1[...], 0, 0)
    g_proj2[...] = dot(dz2[:, :P2], rows_part, 0, 0)


def back_kernel(got, pick, back_t, loss):
    back_t[...] = dot(got[:, :NAR], pick[...], 0, 0)
    terms = dot(got[:, NAR:], pick[...], 0, 0)
    loss[...] = terms[0:1] + terms[1:2] + terms[2:3]


def head_kernel(col, hidden, weight, clusters, out, acc, stat):
    step = pl.program_id(0)

    @pl.when(step == 0)
    def _():
        acc[...] = jnp.zeros_like(acc)
        stat[0:1, :] = jnp.full((1, T), NEG, f32)
        stat[1:2, :] = jnp.zeros((1, T), f32)
        stat[2:3, :] = jnp.zeros((1, T), f32)

    def absorb(block, start, size):
        logits = dot(hidden[...], block[...]).T
        index = iota((size, T), 0) + start
        if size == TAIL:
            logits = jnp.where(index < GW, logits, NEG)
        old = stat[0:1, :]
        top = jnp.maximum(old, jnp.max(logits, axis=0, keepdims=True))
        scale = jnp.exp(old - top)
        terms = jnp.exp(logits - top)
        hot = index == col[...]
        stat[0:1, :] = top
        stat[1:2, :] = stat[1:2, :] * scale + jnp.sum(terms, axis=0, keepdims=True)
        stat[2:3, :] = stat[2:3, :] + jnp.sum(jnp.where(hot, logits, 0.0), axis=0, keepdims=True)
        right = jnp.concatenate([jnp.where(hot, 0.0, terms), hot.astype(f32)], axis=1).astype(bf16)
        new = dot(block[...], right)
        acc[:, :T] = acc[:, :T] * scale + new[:, :T]
        acc[:, T:] = acc[:, T:] + new[:, T:]

    absorb(weight, step * BLK, BLK)

    @pl.when(step == pl.num_programs(0) - 1)
    def _():
        absorb(clusters, HW, TAIL)
        line = iota((SROW, 2 * T), 0)
        stats = jnp.zeros((SROW, 2 * T), f32)
        rows = parts3(stat[0:1, :]) + parts3(stat[1:2, :]) + parts3(stat[2:3, :])
        rows.append(jnp.zeros((1, T), f32))
        for i in range(len(rows) // 2):
            stats = jnp.where(line == i, jnp.concatenate(rows[2 * i : 2 * i + 2], axis=1), stats)
        for g in range(NCH):
            out[g, :NAR, :] = acc[g * NAR : (g + 1) * NAR, :].astype(bf16)
            out[g, NAR:, :] = stats.astype(bf16)


def head_call(col, hidden, weight):
    return pl.pallas_call(
        head_kernel,
        out_shape=jax.ShapeDtypeStruct((NCH, NAR + SROW, 2 * T), bf16),
        grid=(HW // BLK,),
        in_specs=[
            pl.BlockSpec((1, T), lambda i: (0, 0)),
            pl.BlockSpec((T, D), lambda i: (0, 0)),
            pl.BlockSpec((D, BLK), lambda i: (0, i)),
            pl.BlockSpec((D, TAIL), lambda i: (0, HW // TAIL)),
        ],
        out_specs=pl.BlockSpec((NCH, NAR + SROW, 2 * T), lambda i: (0, 0, 0)),
        scratch_shapes=[pltpu.VMEM((D, 2 * T), f32), pltpu.VMEM((8, T), f32)],
        compiler_params=pltpu.CompilerParams(dimension_semantics=("arbitrary",)),
        cost_estimate=pl.CostEstimate(flops=2 * 10**9, bytes_accessed=6 * 10**6, transcendentals=0),
    )(col, hidden, weight, weight)


def conv_kernel(parts, back_t, tail_loss, gates, weight, conv, grad, loss, taps):
    tops, totals, target = [], [], 0.0
    for g in range(NCH):
        stats = parts[g, NAR:, :].astype(f32)
        s3 = [stats[i // 2 : i // 2 + 1, i % 2 * T : (i % 2 + 1) * T] for i in range(9)]
        tops.append(s3[0] + s3[1] + s3[2])
        totals.append(s3[3] + s3[4] + s3[5])
        target = target + (s3[6] + s3[7] + s3[8])
    top = functools.reduce(jnp.maximum, tops)
    scales = [jnp.exp(t - top) for t in tops]
    total = sum(s * t for s, t in zip(scales, totals))
    log_all = top + jnp.log(total)
    inverse = 1.0 / total
    loss[...] = log_all - target + tail_loss[...]
    dh = back_t[...]
    column = jnp.zeros((NAR, T), f32)
    for g in range(NCH):
        dh = dh + parts[g, :NAR, :T].astype(f32) * (scales[g] * inverse)
        column = column + parts[g, :NAR, T:].astype(f32)
    dh = dh + (jnp.exp(target - log_all) - 1.0) * column
    grad[...] = dh
    a = gates[0].astype(f32)
    sig = 1.0 / (1.0 + jnp.exp(-gates[1].astype(f32)))
    da = dh * sig
    db = da * a * (1.0 - sig)
    lane = iota((NAR, T), 1)
    for half, value in enumerate((da, db)):
        for k in range(K):
            moved = value if k == 0 else jnp.where(lane < T - k, pltpu.roll(value, T - k, 1), 0.0)
            at = (half * K + k) * NAR
            taps[at : at + NAR, :] = moved.astype(bf16)
    total_conv = dot(weight[...], taps[...])
    for g in range(NCH):
        conv[g] = total_conv[g * NAR : (g + 1) * NAR].astype(bf16)


def final_kernel(parts, grad, out):
    total = grad[...]
    for g in range(NCH):
        total = total + parts[g].astype(f32)
    out[...] = total.T.astype(bf16)


def on_device(hidden, pre_gates, conv_weight, head_weight, cluster_weight, tail1_proj, tail2_proj, tail1_out, tail2_out, cluster_id, target):
    ch = lax.axis_index("ch").astype(jnp.int32)
    ch_arr = ch.reshape(1)
    (packed,) = call(pack_kernel, [((head_weight.shape[0], HP + CONV), bf16)], head_weight, cluster_weight, conv_weight)
    gathered = lax.all_gather(packed, "tok", axis=0, tiled=True)

    send, pick = call(
        route_kernel,
        [((T, NAR + 128), bf16), ((T, T), bf16)],
        ch_arr,
        cluster_id.reshape(1, T),
        target.reshape(1, T),
        hidden,
        specs=[SMEM] + [VMEM] * 3,
    )
    got = lax.all_to_all(send.reshape(OWN, 2, NAR + 128), "tok", split_axis=0, concat_axis=0, tiled=True).reshape(T, NAR + 128)
    row_parts = lax.all_gather(got[:, :NAR], "ch")
    proj1 = tail1_proj[0]
    proj2 = tail2_proj[0].T
    out1 = tail1_out[0]
    out2 = tail2_out[0]
    feat, part = call(
        tail_kernel,
        [((T, P1), bf16), ((NCH, T, 2 * P1 + 128), bf16)],
        ch_arr, got, row_parts, proj1, proj2, out1, out2,
        specs=[SMEM] + [VMEM] * 6,
        scratch=[pltpu.VMEM((3, T, P1), f32)],
    )
    parts = lax.all_to_all(part, "ch", split_axis=0, concat_axis=0, tiled=True)
    dz1, dz2, log_total, back = call(
        tail_merge_kernel,
        [((T, P1), bf16), ((T, P1), bf16), ((T, 128), f32), ((T, NAR + 128), bf16)],
        ch_arr, got, parts, proj1, proj2,
        specs=[SMEM] + [VMEM] * 4,
    )
    got_back = lax.all_to_all(back.reshape(OWN, 2, NAR + 128), "tok", split_axis=0, concat_axis=0, tiled=True).reshape(T, NAR + 128)
    g_out1, g_out2, g_proj1, g_proj2 = call(
        tail_grad_kernel,
        [((P1, W1), f32), ((P2, W2), f32), ((NAR, P1), f32), ((P2, NAR), f32)],
        ch_arr, got, feat, dz1, dz2, log_total, out1, out2,
        specs=[SMEM] + [VMEM] * 7,
    )
    back_t, tail_loss = call(back_kernel, [((NAR, T), f32), ((1, T), f32)], got_back, pick)

    is_tail = cluster_id >= 0
    word_local = target - ch * HW
    cluster_local = cluster_id - ch * CW
    local = jnp.where(
        is_tail,
        jnp.where((cluster_local >= 0) & (cluster_local < CW), HW + cluster_local, -1),
        jnp.where((word_local >= 0) & (word_local < HW), word_local, -1),
    )
    gathered, back_t = lax.optimization_barrier((gathered, back_t))
    head = head_call(local.reshape(1, T), hidden, gathered)
    head_parts = lax.all_to_all(head, "ch", split_axis=0, concat_axis=0, tiled=True)
    conv, grad, loss = call(
        conv_kernel,
        [((NCH, NAR, T), bf16), ((NAR, T), f32), ((1, T), f32)],
        head_parts, back_t, tail_loss, pre_gates.transpose(0, 2, 1), gathered[:, HP:],
        scratch=[pltpu.VMEM((CONV, T), bf16)],
        limit=LIMIT,
    )
    conv_parts = lax.all_to_all(conv, "ch", split_axis=0, concat_axis=0, tiled=True)
    (grad_input,) = call(final_kernel, [((T, NAR), bf16)], conv_parts, grad, limit=LIMIT)
    return (loss.reshape(T), grad_input, g_proj1[None], g_proj2.T[None], g_out1[None], g_out2[None])


def solution(mesh):
    placed = (
        P("tok", None),
        P(None, "tok", "ch"),
        P(None, None, "tok", "ch"),
        P("tok", "ch"),
        P("tok", "ch"),
        P("tok", None, None),
        P("tok", None, None),
        P("tok", None, "ch"),
        P("tok", None, "ch"),
        P("tok"),
        P("tok"),
    )
    return jax.shard_map(
        on_device,
        mesh=mesh,
        in_specs=placed,
        out_specs=(
            P("tok"),
            P("tok", "ch"),
            P("tok", "ch", None),
            P("tok", "ch", None),
            P("tok", None, "ch"),
            P("tok", None, "ch"),
        ),
        check_vma=False,
    )
```
